256 devices in a mesh: region: 4 (over x), tile: 64 (over y, z, core).
Axes of the slice: x: 4, y: 4, z: 8, core: 2. Of those that a mesh axis runs over, the one named last changes fastest.
Arguments:
- features: bfloat16 [1024, 32, 512], P(('region', 'tile')), may hold values from -6 to 6
- voxel_mask: int32 [1024, 512], P(('region', 'tile')), may hold values 0 or 1
- brick_cell: int32 [1024], P(('region', 'tile')), may hold values from -1 to 7, as said below
- conv_one: bfloat16 [27, 32, 32], replicated, may hold values from -0.3125 to 0.3125
- conv_two: bfloat16 [27, 32, 32], replicated, may hold values from -0.3125 to 0.3125
- down_weight: bfloat16 [8, 32, 64], replicated, may hold values from -0.375 to 0.375
- cotangent: bfloat16 [1024, 4096], P(('region', 'tile')), may hold values from -6 to 6
Outputs:
- down: bfloat16 [1024, 4096], P(('region', 'tile'))
- grad_features: bfloat16 [1024, 32, 512], P(('region', 'tile'))
- grad_conv_one: float32 [27, 32, 32], replicated
- grad_conv_two: float32 [27, 32, 32], replicated
- grad_down: float32 [8, 32, 64], replicated
The draws below stay inside these ranges and needn't reach their ends.
Inputs may be any that keep to these rules, and one draw needn't show every extreme that they name: `brick_cell`: entries come in blocks of 4, one block a device in the order of the slots. The live entries of a block name distinct brick cells of that device's box; -1 marks an empty slot, and in at least one block every entry is live.
All inputs are finite; a program needn't handle non-finite values. No bound on the sum of `voxel_mask` on one device may be relied on, other than what follows from the above.
Results may differ from the reference program's by a relative error of at most 0.0053.
Values may be sent and summed in bfloat16 or wider, within the bound.
A program may use at most 192 MiB of HBM per device.

```python
import jax
import jax.numpy as jnp
from jax import lax

CHANNELS = 32
DOWN_CH = 64
BR_DEV = 4
TOTAL_BRICKS = 1024
N_REGION = 4
N_TILE = 64


def draw_brick_cell(key, part):
    device_count = TOTAL_BRICKS // BR_DEV
    key_count, key_full, key_cells, key_slots = jax.random.split(key, 4)
    lowest = max(BR_DEV // 4, 1)
    counts = jax.random.randint(key_count, (device_count,), lowest, BR_DEV + 1)
    fullest = jax.random.randint(key_full, (), 0, device_count)
    counts = jnp.where(jnp.arange(device_count) == fullest, BR_DEV, counts)
    cell_scores = jax.random.randint(key_cells, (device_count, 2 * BR_DEV), 0, 1 << 20) * (2 * BR_DEV) + jnp.arange(2 * BR_DEV)[None, :]
    chosen = jnp.argsort(cell_scores, axis=1)[:, :BR_DEV]
    slot_scores = jax.random.randint(key_slots, (device_count, BR_DEV), 0, 1 << 20) * BR_DEV + jnp.arange(BR_DEV)[None, :]
    slot_rank = jnp.argsort(jnp.argsort(slot_scores, axis=1), axis=1)
    cell_list = jnp.where(slot_rank < counts[:, None], chosen, -1)
    return cell_list.reshape(-1).astype(jnp.int32)


def place_ends(result, key, smallest, high):
    place = [jax.random.randint(jax.random.fold_in(key, axis), (), 0, length) for axis, length in enumerate(result.shape)]
    main_axis = result.shape.index(max(result.shape))
    next_to = place[:main_axis] + [(place[main_axis] + 1) % result.shape[main_axis]] + place[main_axis + 1:]
    return result.at[tuple(place)].set(smallest).at[tuple(next_to)].set(high)


def block_levels(stream_key, shape, cuts, smallest, high):
    level, own = 1.0, jax.random.fold_in(stream_key, 6)
    for position, shards_of in cuts:
        steps = jnp.exp(jax.random.uniform(jax.random.fold_in(own, position), (shards_of,), jnp.float32, smallest / len(cuts), high / len(cuts)))
        level = level * jnp.repeat(steps, shape[position] // shards_of).reshape([-1 if axis == position else 1 for axis in range(len(shape))])
    return level


def scatter_about(rng, extent, scale, reach, cuts=(), held_as=jnp.bfloat16):
    factor_of = block_levels(rng, extent, cuts, -0.22, 0.18) if cuts else 1.0
    values = jax.random.normal(rng, extent, jnp.float32) * scale * factor_of
    return jnp.minimum(jnp.maximum(values, -reach), reach).astype(held_as)


def setup_inputs(seed: int = 0) -> dict:
    key_list = jax.random.split(jax.random.key(seed), 8)
    features = scatter_about(key_list[0], (TOTAL_BRICKS, CHANNELS, 512), 1.0, 6.0, ((0, 256),))
    voxel_mask = place_ends((jax.random.randint(key_list[1], (TOTAL_BRICKS, 512), 0, 4) < 3).astype(jnp.int32), jax.random.fold_in(key_list[1], 1), 0, 1)
    brick_cell = draw_brick_cell(jax.random.fold_in(key_list[7], 71), 0)
    conv_one = scatter_about(key_list[3], (27, CHANNELS, CHANNELS), (13 * CHANNELS) ** -0.5, 0.3125)
    conv_two = scatter_about(key_list[4], (27, CHANNELS, CHANNELS), (13 * CHANNELS) ** -0.5, 0.3125)
    down_weight = scatter_about(key_list[5], (8, CHANNELS, DOWN_CH), (8 * CHANNELS) ** -0.5, 0.375)
    cotangent = scatter_about(key_list[6], (TOTAL_BRICKS, DOWN_CH * 64), 1.0, 6.0, ((0, 256),))
    return dict(features=features, voxel_mask=voxel_mask, brick_cell=brick_cell, conv_one=conv_one, conv_two=conv_two, down_weight=down_weight, cotangent=cotangent)


def global_tables(brick_cell):
    slot_ids = jnp.arange(TOTAL_BRICKS, dtype=jnp.int32)
    device_ids = slot_ids // BR_DEV
    region_ids = device_ids // N_TILE
    tile_ids = device_ids % N_TILE
    live_slot = brick_cell >= 0
    cell_index = jnp.maximum(brick_cell, 0)
    brick_x = 2 * region_ids + cell_index // BR_DEV
    brick_z = cell_index % BR_DEV
    size_y = 8 * N_TILE + 2
    size_z = 8 * BR_DEV + 2
    voxel_index = jnp.arange(512, dtype=jnp.int32)
    global_x = 8 * brick_x[:, None] + voxel_index[None, :] // 64
    global_y = 8 * tile_ids[:, None] + voxel_index[None, :] // 8 % 8
    global_z = 8 * brick_z[:, None] + voxel_index[None, :] % 8
    base_index = ((global_x + 1) * size_y + global_y + 1) * size_z + global_z + 1
    offsets = [(shift_x * size_y + shift_y) * size_z + shift_z for shift_x in (-1, 0, 1) for shift_y in (-1, 0, 1) for shift_z in (-1, 0, 1)]
    grid_owner = jnp.full((2 * N_REGION, N_TILE, BR_DEV), TOTAL_BRICKS, dtype=jnp.int32)
    grid_owner = grid_owner.at[jnp.where(live_slot, brick_x, 2 * N_REGION), tile_ids, brick_z].set(slot_ids, mode='drop')
    return (live_slot, base_index, jnp.array(offsets, dtype=jnp.int32), grid_owner)

def global_field(values, grid_owner):
    channel_count = values.shape[1]
    padding = jnp.zeros((1, channel_count, 512), values.dtype)
    bricks = jnp.concatenate([values, padding], axis=0)[grid_owner]
    bricks = bricks.reshape(2 * N_REGION, N_TILE, BR_DEV, channel_count, 8, 8, 8)
    bricks = bricks.transpose(3, 0, 4, 1, 5, 2, 6)
    field = bricks.reshape(channel_count, 16 * N_REGION, 8 * N_TILE, 8 * BR_DEV)
    field = jnp.pad(field, ((0, 0), (1, 1), (1, 1), (1, 1)))
    return field.reshape(channel_count, -1)

def device_blocks(base_index):
    return base_index.reshape(TOTAL_BRICKS // BR_DEV, BR_DEV * 512)

def apply_conv(flat, base_index, offsets, weights, sign):
    weights_wide = weights.astype(jnp.float32)

    def one_block(block_index):
        index_all = (block_index[None, :] + sign * offsets[:, None]).reshape(-1)
        columns = jnp.take(flat, index_all, axis=1).reshape(flat.shape[0], 27, -1).astype(jnp.float32)
        if sign > 0:
            return jnp.einsum('ikn,kio->on', columns, weights_wide)
        return jnp.einsum('okn,kio->in', columns, weights_wide)
    planes = lax.map(one_block, device_blocks(base_index))
    count = planes.shape[1]
    planes = planes.reshape(TOTAL_BRICKS // BR_DEV, count, BR_DEV, 512).transpose(0, 2, 1, 3)
    return planes.reshape(TOTAL_BRICKS, count, 512)

def weight_grad(flat, base_index, offsets, grads):
    count = grads.shape[1]
    grad_blocks = grads.reshape(TOTAL_BRICKS // BR_DEV, BR_DEV, count, 512).transpose(0, 2, 1, 3)
    grad_blocks = grad_blocks.reshape(TOTAL_BRICKS // BR_DEV, count, BR_DEV * 512)

    def add_block(total, pair):
        block_index, block_grad = pair
        index_all = (block_index[None, :] + offsets[:, None]).reshape(-1)
        columns = jnp.take(flat, index_all, axis=1).reshape(flat.shape[0], 27, -1).astype(jnp.float32)
        return (total + jnp.einsum('ikn,on->kio', columns, block_grad.astype(jnp.float32)), None)
    start = jnp.zeros((27, flat.shape[0], count), jnp.float32)
    total, _ = lax.scan(add_block, start, (device_blocks(base_index), grad_blocks))
    return total

def reference(features, voxel_mask, brick_cell, conv_one, conv_two, down_weight, cotangent):
    live_slot, base_index, offsets, grid_owner = global_tables(brick_cell)
    mask_slot = (voxel_mask.astype(jnp.float32) * live_slot[:, None].astype(jnp.float32))[:, None, :]
    inputs = features * mask_slot.astype(jnp.bfloat16)
    input_flat = global_field(inputs, grid_owner)
    first_pre = apply_conv(input_flat, base_index, offsets, conv_one, 1) * mask_slot
    hidden = jax.nn.silu(first_pre).astype(jnp.bfloat16)
    hidden_flat = global_field(hidden, grid_owner)
    second_pre = apply_conv(hidden_flat, base_index, offsets, conv_two, 1) * mask_slot
    summed = (inputs.astype(jnp.float32) + second_pre).astype(jnp.bfloat16)
    shaped = summed.reshape(TOTAL_BRICKS, CHANNELS, 4, 2, 4, 2, 4, 2).astype(jnp.float32)
    kernel = down_weight.reshape(2, 2, 2, CHANNELS, DOWN_CH).astype(jnp.float32)
    down = jnp.einsum('tcxaybzd,abdco->toxyz', shaped, kernel).reshape(TOTAL_BRICKS, -1).astype(jnp.bfloat16)
    upstream = cotangent.reshape(TOTAL_BRICKS, DOWN_CH, 4, 4, 4).astype(jnp.float32)
    back_sum = jnp.einsum('toxyz,abdco->tcxaybzd', upstream, kernel).reshape(TOTAL_BRICKS, CHANNELS, 512)
    down_grad = jnp.einsum('tcxaybzd,toxyz->abdco', shaped, upstream).reshape(8, CHANNELS, DOWN_CH)
    second_grad = (back_sum * mask_slot).astype(jnp.bfloat16)
    grad_flat = global_field(second_grad, grid_owner)
    weight_two = weight_grad(hidden_flat, base_index, offsets, second_grad)
    spread = apply_conv(grad_flat, base_index, offsets, conv_two, -1)
    sigmoid_value = jax.nn.sigmoid(first_pre)
    first_grad = (spread * sigmoid_value * (1.0 + first_pre * (1.0 - sigmoid_value)) * mask_slot).astype(jnp.bfloat16)
    first_flat = global_field(first_grad, grid_owner)
    weight_one = weight_grad(input_flat, base_index, offsets, first_grad)
    input_grad = (back_sum + apply_conv(first_flat, base_index, offsets, conv_one, -1)) * mask_slot
    scale = (TOTAL_BRICKS * 512.0) ** (-0.5)
    return (down, input_grad.astype(jnp.bfloat16), weight_one * scale, weight_two * scale, down_grad * scale)
```

```python
import math

import jax
import jax.numpy as jnp
from jax import lax
from jax.experimental import pallas as pl
from jax.experimental.pallas import tpu as pltpu
from jax.sharding import PartitionSpec as P

MESH = pl.DeviceIdType.MESH
F32 = jnp.float32
BF16 = jnp.bfloat16
NT = (((1,), (1,)), ((), ()))
TN = (((0,), (0,)), ((), ()))


def mm(a, b):
    return jnp.dot(a, b, preferred_element_type=F32)


def mmd(a, b, dims):
    return lax.dot_general(a, b, dims, preferred_element_type=F32)


def iota(shape, dim):
    return lax.broadcasted_iota(jnp.int32, shape, dim)


def one_hot(cond):
    return jnp.where(cond, 1.0, 0.0)


def shift_z(rows, amount):
    count = rows.shape[0]
    z = iota(rows.shape, 0) % 32
    rolled = pltpu.roll(rows, (-amount) % count, 0)
    keep = (z < 31) if amount > 0 else (z > 0)
    return jnp.where(keep, rolled, 0.0)


def put_center(fk, first_x, rows):
    n = rows.shape[0] // 32
    for k, amount in enumerate((-1, 0, 1)):
        moved = rows if amount == 0 else shift_z(rows, amount)
        fk[pl.ds(first_x, n), :, 256 * k : 256 * k + 256] = moved.astype(BF16).reshape(n, 32, 256)


def pack_edge(rows, lane0, lanes):
    n = rows.shape[0] // 32
    cube = rows.reshape(n, 4, 8, 128)
    total = None
    for zb in range(4):
        part = cube[:, zb].reshape(n * 8, 128)
        turn = (32 * zb - lane0) % 128
        if turn:
            part = pltpu.roll(part, turn, 1)
        total = part if total is None else jnp.where(lanes // 32 == zb, part, total)
    return total


def put_edges(fk, first_x, low, high, vscr):
    n = low.shape[0] // 8
    lane = iota((n * 8, 128), 1)
    for zb in range(4):
        a = low if zb == 0 else pltpu.roll(low, (-32 * zb) % 128, 1)
        turn = (32 - 32 * zb) % 128
        b = high if turn == 0 else pltpu.roll(high, turn, 1)
        v = jnp.where(lane < 32, a, jnp.where(lane < 64, b, 0.0))
        vscr[0:n, 8 * zb : 8 * zb + 8, :] = v.reshape(n, 8, 128)
    v = vscr[0:n].reshape(n * 32, 128)
    first = shift_z(v, -1) + pltpu.roll(v, 64, 1)
    fk[pl.ds(first_x, n), :, 768:896] = first.astype(BF16).reshape(n, 32, 128)
    fk[pl.ds(first_x, n), :, 896:1024] = shift_z(v, 1).astype(BF16).reshape(n, 32, 128)


def conv(fk, t_ref, kind, out):
    for part in range(2):
        total = None
        for dx in range(3):
            lhs = fk[dx + 8 * part : dx + 8 * part + 8].reshape(256, 1024)
            term = mm(lhs, t_ref[kind, dx])
            total = term if total is None else total + term
        out[256 * part : 256 * part + 256, :] = total


def kernel_grad(xt, fk, mscr, blocks):
    lane = iota((32, 256), 1)
    for dx in range(3):
        rhs = fk[dx : dx + 16].reshape(512, 1024)
        mscr[...] = mm(xt, rhs)
        for dz in range(3):
            total = None
            for j in range(8):
                piece = mscr[32 * j : 32 * j + 32, 256 * dz : 256 * dz + 256]
                if j in (0, 7):
                    edge = mscr[32 * j : 32 * j + 32, 768:1024]
                    have = 64 * dz + (0 if j == 0 else 32)
                    want = 224 if j == 0 else 0
                    turn = (want - have) % 256
                    if turn:
                        edge = pltpu.roll(edge, turn, 1)
                    piece = jnp.where(lane // 32 == want // 32, edge, piece)
                turn = (32 - 32 * j) % 256
                if turn:
                    piece = pltpu.roll(piece, turn, 1)
                total = piece if total is None else total + piece
            blocks[3 * dx + dz] = total[:, 0:128]


def pack_blocks(blocks, dst, first):
    lane = iota((32, 128), 1)
    for g in range(7):
        value = blocks[g]
        if g < 6:
            extra = pltpu.roll(blocks[7 + g // 3], 32 * (3 - g % 3), 1)
            value = jnp.where(lane < 96, value, extra)
        dst[first + 32 * g : first + 32 * g + 32, :] = value.astype(BF16)


def build(n_r, n_t):
    inner = min(16, n_t)
    outer = n_t // inner
    g1 = n_r * outer
    g2 = inner
    rows_w = 512 // g1
    rows_d = 128 // g1
    scale = 1.0 / math.sqrt(4 * n_r * n_t * 512.0)

    def body(
        bc, feat, vmask, cot, wcat, dwn, dwt,
        o_down, o_gf, o_w1, o_w2, o_wd,
        tmats, wtile, wdn, wback, pick, pslot, mslot, cslot,
        maskd, dense, inpd, backd, crow, fki, fkg, fkh, fkf, pre, acc, mscr, vscr, blocks, stage,
        sx, sy, sc, rx, ry, rc,
        pw, p1, q1, p2, q2, p3, q3, pd, d1, e1, d2, e2, d3, e3,
        hs, hr, w1s, w1r, w2s, w2r, w3s, w3r, d1s, d1r, d2s, d2r, d3s, d3r,
    ):
        r = lax.axis_index("region")
        t = lax.axis_index("tile")
        y = t // inner
        u = t % inner
        m = r * outer + y

        def peer1(k):
            return (k // outer, (k % outer) * inner + u)

        def peer2(k):
            return (r, y * inner + k)

        near = [(dr, dt) for dr in (-1, 0, 1) for dt in (-1, 0, 1) if (dr, dt) != (0, 0)]

        def neighbour(dr, dt):
            return ((r + dr + n_r) % n_r, (t + dt + n_t) % n_t)

        barrier = pltpu.get_barrier_semaphore()
        for dr, dt in near:
            pl.semaphore_signal(barrier, inc=1, device_id=neighbour(dr, dt), device_id_type=MESH)

        def greet1(k, carry):
            pl.semaphore_signal(barrier, inc=1, device_id=peer1((m + k) % g1), device_id_type=MESH)
            return carry

        def greet2(k, carry):
            pl.semaphore_signal(barrier, inc=1, device_id=peer2((u + k) % g2), device_id_type=MESH)
            return carry

        lax.fori_loop(1, g1, greet1, 0)
        lax.fori_loop(1, g2, greet2, 0)

        v = iota((64, 512), 1)
        w = iota((64, 512), 0)
        pick[...] = one_hot((v // 64 == w // 8) & (v % 8 == w % 8)).astype(BF16)
        jv = iota((256, 512), 1) // 8 % 8
        jr = iota((256, 512), 0) // 32
        jmask = one_hot(jv == jr).astype(BF16)
        cv = iota((32, 64), 1)
        cw = iota((32, 64), 0)
        up = one_hot((cv // 16 == cw // 8) & (cv % 4 == cw % 8 // 2)).astype(BF16)
        even = one_hot((cv // 16 == cw // 8) & (2 * (cv % 4) == cw % 8)).astype(BF16)
        ymask = one_hot(iota((256, 64), 1) // 4 % 4 == iota((256, 64), 0) // 64).astype(BF16)

        pslot[4] = jnp.zeros((64, 256), F32)
        mslot[4] = jnp.zeros((64, 256), F32)
        cslot[4] = jnp.zeros((32, 256), F32)
        for s in range(4):
            tall = jnp.concatenate([feat[s]] * 8, axis=0) * jmask
            pslot[s] = mmd(pick[...], tall, NT)
            lanes = jnp.broadcast_to(vmask[pl.ds(s, 1), :].astype(F32), (256, 512)).astype(BF16)
            mslot[s] = mmd(pick[...], lanes * jmask, NT)
            tall = jnp.concatenate([cot[s]] * 4, axis=0) * ymask
            cslot[s] = mmd(up, tall, NT)
        for e in range(8):
            owner = jnp.int32(4)
            for s in range(4):
                owner = jnp.where(bc[s] == e, jnp.int32(s), owner)
            xb, zb = e // 4, e % 4
            mk = mslot[owner]
            maskd[8 * xb : 8 * xb + 8, zb] = mk.reshape(8, 8, 256)
            inpd[8 * xb : 8 * xb + 8, zb] = (pslot[owner] * mk).reshape(8, 8, 256)
            crow[4 * xb : 4 * xb + 4, zb] = cslot[owner].reshape(4, 8, 256)

        rep = one_hot(iota((64, 256), 1) % 64 == iota((64, 256), 0)).astype(BF16)
        dtile = mm(dwn[...], rep)
        lane64 = iota((32, 256), 1) // 64
        for a in range(2):
            for b in range(2):
                for d in range(2):
                    k = 4 * a + 2 * b + d
                    block = dtile[32 * k : 32 * k + 32]
                    for y4 in range(4):
                        row = 256 * a + 32 * (2 * y4 + b)
                        wdn[row : row + 32, 256 * d : 256 * d + 256] = jnp.where(
                            lane64 == y4, block, 0.0
                        ).astype(BF16)
        btile = mm(dwt[...], rep)
        lane64 = iota((64, 256), 1) // 64
        for ad in range(4):
            block = btile[64 * ad : 64 * ad + 64]
            for y4 in range(4):
                wback[64 * y4 : 64 * y4 + 64, 256 * ad : 256 * ad + 256] = jnp.where(
                    lane64 == y4, block, 0.0
                ).astype(BF16)

        crow_b = crow[...].reshape(256, 256).astype(BF16)
        odd = iota((256, 256), 0) % 2 == 1
        for a in range(2):
            back = jnp.where(
                odd,
                mm(crow_b, wback[:, 512 * a + 256 : 512 * a + 512]),
                mm(crow_b, wback[:, 512 * a : 512 * a + 256]),
            ).reshape(8, 32, 256)
            for x4 in range(8):
                backd[2 * x4 + a] = back[x4]

        lane_e = iota((64, 128), 1)

        def send_pack(phase, field, rows, at):
            low = pack_edge(rows[:, 0:128], 0, iota((64, 128), 1))
            high = pack_edge(rows[:, 128:256], 96, iota((64, 128), 1))
            sy[phase, 0, field, 8 * at : 8 * at + 64, :] = low.astype(BF16)
            sy[phase, 1, field, 8 * at : 8 * at + 64, :] = high.astype(BF16)
            if at == 0:
                sx[phase, 0, field] = rows[0:32].astype(BF16)
                sc[phase, 0, field] = low[0:8].astype(BF16)
                sc[phase, 1, field] = high[0:8].astype(BF16)
            else:
                sx[phase, 1, field] = rows[224:256].astype(BF16)
                sc[phase, 2, field] = low[56:64].astype(BF16)
                sc[phase, 3, field] = high[56:64].astype(BF16)

        for part in range(2):
            at = 8 * part
            rows = inpd[at : at + 8].reshape(256, 256)
            put_center(fki, 1 + at, rows)
            send_pack(0, 0, rows, at)
            rows = backd[at : at + 8].reshape(256, 256) * maskd[at : at + 8].reshape(256, 256)
            rows = rows.astype(BF16).astype(F32)
            put_center(fkg, 1 + at, rows)
            send_pack(0, 1, rows, at)

        pl.semaphore_wait(barrier, 8 + (g1 - 1) + (g2 - 1))

        def halo(phase):
            copies = []
            plan = [
                (sx.at[phase, 0], rx.at[phase, 1], (-1, 0)),
                (sx.at[phase, 1], rx.at[phase, 0], (1, 0)),
                (sy.at[phase, 0], ry.at[phase, 1], (0, -1)),
                (sy.at[phase, 1], ry.at[phase, 0], (0, 1)),
                (sc.at[phase, 0], rc.at[phase, 3], (-1, -1)),
                (sc.at[phase, 1], rc.at[phase, 2], (-1, 1)),
                (sc.at[phase, 2], rc.at[phase, 1], (1, -1)),
                (sc.at[phase, 3], rc.at[phase, 0], (1, 1)),
            ]
            for k, (src, dst, (dr, dt)) in enumerate(plan):
                copies.append(
                    pltpu.make_async_remote_copy(
                        src_ref=src,
                        dst_ref=dst,
                        send_sem=hs.at[phase, k],
                        recv_sem=hr.at[phase, k],
                        device_id=neighbour(dr, dt),
                        device_id_type=MESH,
                    )
                )
            return copies

        has = [
            jnp.where(r > 0, 1.0, 0.0),
            jnp.where(r < n_r - 1, 1.0, 0.0),
            jnp.where(t > 0, 1.0, 0.0),
            jnp.where(t < n_t - 1, 1.0, 0.0),
        ]

        def put_halo(phase, field, fk):
            put_center(fk, 0, rx[phase, 0, field].astype(F32) * has[0])
            put_center(fk, 17, rx[phase, 1, field].astype(F32) * has[1])
            for part in range(2):
                rows = slice(64 * part, 64 * part + 64)
                put_edges(
                    fk,
                    1 + 8 * part,
                    ry[phase, 0, field, rows].astype(F32) * has[2],
                    ry[phase, 1, field, rows].astype(F32) * has[3],
                    vscr,
                )
            for side in range(2):
                put_edges(
                    fk,
                    17 * side,
                    rc[phase, 2 * side, field].astype(F32) * (has[side] * has[2]),
                    rc[phase, 2 * side + 1, field].astype(F32) * (has[side] * has[3]),
                    vscr,
                )

        first = halo(0)
        for c in first:
            c.start()

        rep32 = one_hot(iota((32, 256), 1) % 32 == iota((32, 256), 0)).astype(BF16)
        wtile[...] = mm(wcat[...], rep32).astype(BF16)
        jl = iota((32, 256), 1) // 32
        masks = [one_hot(jl == j).astype(BF16) for j in range(8)]
        nothing = jnp.zeros((32, 256), BF16)

        def band(kind, carry):
            for dx in range(3):
                for dz in range(3):
                    low, mid, high = (
                        wtile[pl.ds(pl.multiple_of(864 * kind + 32 * (9 * dx + 3 * dy + dz), 32), 32), :]
                        for dy in range(3)
                    )
                    for j in range(8):
                        value = mid * masks[j]
                        if j > 0:
                            value = value + high * masks[j - 1]
                        if j < 7:
                            value = value + low * masks[j + 1]
                        tmats[kind, dx, 256 * dz + 32 * j : 256 * dz + 32 * j + 32, :] = value
                    at = 768 + 64 * dz
                    tmats[kind, dx, at : at + 32, :] = low * masks[0]
                    tmats[kind, dx, at + 32 : at + 64, :] = high * masks[7]
                tmats[kind, dx, 960:992, :] = nothing
                tmats[kind, dx, 992:1024, :] = nothing
            return carry

        lax.fori_loop(0, 4, band, 0)

        for c in first:
            c.wait_recv()
        put_halo(0, 0, fki)
        put_halo(0, 1, fkg)

        conv(fki, tmats, 0, pre)
        conv(fkg, tmats, 3, acc)

        for part in range(2):
            at = 8 * part
            rows = slice(256 * part, 256 * part + 256)
            mk = maskd[at : at + 8].reshape(256, 256)
            before = pre[rows] * mk
            sig = 1.0 / (1.0 + jnp.exp(-before))
            hidden = (before / (1.0 + jnp.exp(-before))).astype(BF16).astype(F32)
            put_center(fkh, 1 + at, hidden)
            send_pack(1, 0, hidden, at)
            grad = acc[rows] * sig * (1.0 + before * (1.0 - sig)) * mk
            grad = grad.astype(BF16).astype(F32)
            put_center(fkf, 1 + at, grad)
            send_pack(1, 1, grad, at)

        second = halo(1)
        for c in second:
            c.start()

        stage[...] = fkf[1:17, :, 256:512].reshape(512, 256).T
        kernel_grad(stage[...], fki, mscr, blocks)
        pack_blocks(blocks, pw, 0)
        stage[...] = fkh[1:17, :, 256:512].reshape(512, 256).T
        kernel_grad(stage[...], fkg, mscr, blocks)
        pack_blocks(blocks, pw, 224)
        pw[448:480, :] = jnp.zeros((32, 128), BF16)
        pw[480:512, :] = jnp.zeros((32, 128), BF16)
        for k in range(g1):
            p1[k] = pw[rows_w * k : rows_w * k + rows_w, :]
        q1[m] = p1[m]

        def start_all(src, dst, mine, count, peer, send, recv, by_peer):
            def go(k, carry):
                other = (mine + k) % count
                pltpu.make_async_remote_copy(
                    src_ref=src.at[other] if by_peer else src,
                    dst_ref=dst.at[mine],
                    send_sem=send.at[k],
                    recv_sem=recv.at[k],
                    device_id=peer(other),
                    device_id_type=MESH,
                ).start()
                return carry

            lax.fori_loop(1, count, go, 0)

        def wait_all(src, dst, mine, count, peer, send, recv, by_peer):
            def go(k, carry):
                other = (mine + count - k) % count
                c = pltpu.make_async_remote_copy(
                    src_ref=src.at[other] if by_peer else src,
                    dst_ref=dst.at[other],
                    send_sem=send.at[k],
                    recv_sem=recv.at[k],
                    device_id=peer(other),
                    device_id_type=MESH,
                )
                c.wait_recv()
                c.wait_send()
                return carry

            lax.fori_loop(1, count, go, 0)

        plan_w1 = (p1, q1, m, g1, peer1, w1s, w1r, True)
        plan_w2 = (p2, q2, u, g2, peer2, w2s, w2r, False)
        plan_w3 = (p3, q3, m, g1, peer1, w3s, w3r, False)
        plan_d1 = (d1, e1, m, g1, peer1, d1s, d1r, True)
        plan_d2 = (d2, e2, u, g2, peer2, d2s, d2r, False)
        plan_d3 = (d3, e3, m, g1, peer1, d3s, d3r, False)

        def added(ref, count):
            total = ref[0].astype(F32)
            for k in range(1, count):
                total = total + ref[k].astype(F32)
            return total

        start_all(*plan_w1)

        for c in second:
            c.wait_recv()
        put_halo(1, 0, fkh)
        conv(fkh, tmats, 1, acc)
        for x in range(16):
            dense[x] = (inpd[x].reshape(32, 256) + acc[32 * x : 32 * x + 32, :] * maskd[x].reshape(32, 256)).astype(BF16)

        stage[...] = dense[...].reshape(512, 256).T
        odd_x = iota((256, 256), 0) % 2 == 1
        crow_rows = crow[...].reshape(256, 256)
        half = [jnp.where(odd_x, 0.0, crow_rows).astype(BF16), jnp.where(odd_x, crow_rows, 0.0).astype(BF16)]
        crow_up = [
            jnp.broadcast_to(h.reshape(8, 1, 32, 256), (8, 2, 32, 256)).reshape(16, 32, 256) for h in half
        ]
        xpar = iota((512, 256), 0) // 32 % 2
        low64 = iota((64, 128), 1) < 64
        for a in range(2):
            halves = []
            for d in range(2):
                full = jnp.where(xpar == a, crow_up[d].reshape(512, 256).astype(F32), 0.0).astype(BF16)
                mscr[:, 0:256] = mm(stage[...], full)
                even_part = mscr[0:64, 0:128] + mscr[128:192, 128:256]
                odd_part = mscr[64:128, 0:128] + mscr[192:256, 128:256]
                if d == 0:
                    halves.append(even_part + pltpu.roll(odd_part, 64, 1))
                else:
                    halves.append(pltpu.roll(even_part, 64, 1) + odd_part)
            pd[64 * a : 64 * a + 64, :] = jnp.where(low64, halves[0], halves[1])
        for k in range(g1):
            d1[k] = pd[rows_d * k : rows_d * k + rows_d, :]
        e1[m] = d1[m]
        start_all(*plan_d1)

        even_x = jnp.concatenate([dense[2 * k].reshape(1, 32, 256) for k in range(8)], axis=0)
        odd_x2 = jnp.concatenate([dense[2 * k + 1].reshape(1, 32, 256) for k in range(8)], axis=0)
        lhs = jnp.concatenate([even_x.reshape(256, 256), odd_x2.reshape(256, 256)], axis=1)
        acc[0:256, :] = mm(lhs, wdn[:, 0:256]) + pltpu.roll(mm(lhs, wdn[:, 256:512]), 255, 0)
        for k in range(8):
            for zb in range(4):
                crow[k, zb] = acc[32 * k + 8 * zb : 32 * k + 8 * zb + 8, :]
        for s in range(4):
            e = jnp.maximum(bc[s], 0)
            live = jnp.where(bc[s] >= 0, 1.0, 0.0)
            got = (crow[pl.ds(4 * (e // 4), 4), e % 4].reshape(32, 256) * live).astype(BF16)
            wide = mmd(got, even, TN)
            total = None
            for y4 in range(4):
                part = jnp.where(iota((64, 64), 1) // 4 % 4 == y4, wide[64 * y4 : 64 * y4 + 64], 0.0)
                total = part if total is None else total + part
            o_down[s] = total.astype(BF16)

        wait_all(*plan_w1)
        p2[...] = added(q1, g1).astype(BF16)
        q2[u] = p2[...]
        start_all(*plan_w2)

        put_halo(1, 1, fkf)
        conv(fkf, tmats, 2, acc)

        wait_all(*plan_d1)
        d2[...] = added(e1, g1)
        e2[u] = d2[...]
        start_all(*plan_d2)

        for x in range(16):
            value = (backd[x] + acc[32 * x : 32 * x + 32, :]) * maskd[x].reshape(32, 256)
            inpd[x] = value.reshape(4, 8, 256)
        jl512 = iota((32, 512), 1) // 8 % 8
        for s in range(4):
            e = jnp.maximum(bc[s], 0)
            live = jnp.where(bc[s] >= 0, 1.0, 0.0)
            got = (inpd[pl.ds(8 * (e // 4), 8), e % 4].reshape(64, 256) * live).astype(BF16)
            wide = mmd(got, pick[...], TN)
            total = None
            for j in range(8):
                part = jnp.where(jl512 == j, wide[32 * j : 32 * j + 32], 0.0)
                total = part if total is None else total + part
            o_gf[s] = total.astype(BF16)

        wait_all(*plan_w2)
        p3[...] = (added(q2, g2) * scale).astype(BF16)
        q3[m] = p3[...]
        start_all(*plan_w3)
        wait_all(*plan_d2)
        d3[...] = added(e2, g2) * scale
        e3[m] = d3[...]
        start_all(*plan_d3)

        wait_all(*plan_w3)
        for k in range(g1):
            pw[rows_w * k : rows_w * k + rows_w, :] = q3[k]

        def tap_of(group, slot):
            block, dy = (group, slot) if slot < 3 else (7 + group // 3, group % 3)
            return 9 * (block // 3) + 3 * dy + block % 3

        for g in range(7):
            one = pw[32 * g : 32 * g + 32, :].astype(F32).T
            two = pw[224 + 32 * g : 224 + 32 * g + 32, :].astype(F32)
            for slot in range(4 if g < 6 else 3):
                k = tap_of(g, slot)
                o_w1[k] = one[32 * slot : 32 * slot + 32, :]
                o_w2[26 - k] = two[:, 32 * slot : 32 * slot + 32]

        wait_all(*plan_d3)
        for k in range(g1):
            pd[rows_d * k : rows_d * k + rows_d, :] = e3[k]
        for a in range(2):
            for b in range(2):
                for d in range(2):
                    o_wd[4 * a + 2 * b + d] = pd[
                        64 * a + 32 * b : 64 * a + 32 * b + 32, 64 * d : 64 * d + 64
                    ]
        for c in first + second:
            c.wait_send()

    def vm(shape, dtype=F32):
        return pltpu.VMEM(shape, dtype)

    dma = pltpu.SemaphoreType.DMA
    scratch = [
        vm((4, 3, 1024, 256), BF16), vm((3456, 256), BF16), vm((512, 512), BF16), vm((256, 1024), BF16),
        vm((64, 512), BF16), vm((5, 64, 256)), vm((5, 64, 256)), vm((5, 32, 256)),
        vm((16, 4, 8, 256)), vm((16, 32, 256), BF16), vm((16, 4, 8, 256)), vm((16, 32, 256)), vm((8, 4, 8, 256)),
        vm((18, 32, 1024), BF16), vm((18, 32, 1024), BF16), vm((18, 32, 1024), BF16), vm((18, 32, 1024), BF16),
        vm((512, 256)), vm((512, 256)), vm((256, 1024)), vm((8, 32, 128)), vm((9, 32, 128)), vm((256, 512), BF16),
        vm((2, 2, 2, 32, 256), BF16), vm((2, 2, 2, 128, 128), BF16), vm((2, 4, 2, 8, 128), BF16),
        vm((2, 2, 2, 32, 256), BF16), vm((2, 2, 2, 128, 128), BF16), vm((2, 4, 2, 8, 128), BF16),
        vm((512, 128), BF16), vm((g1, rows_w, 128), BF16), vm((g1, rows_w, 128), BF16),
        vm((rows_w, 128), BF16), vm((g2, rows_w, 128), BF16), vm((rows_w, 128), BF16), vm((g1, rows_w, 128), BF16),
        vm((128, 128)), vm((g1, rows_d, 128)), vm((g1, rows_d, 128)),
        vm((rows_d, 128)), vm((g2, rows_d, 128)), vm((rows_d, 128)), vm((g1, rows_d, 128)),
        dma((2, 8)), dma((2, 8)),
        dma((g1,)), dma((g1,)), dma((g2,)), dma((g2,)), dma((g1,)), dma((g1,)),
        dma((g1,)), dma((g1,)), dma((g2,)), dma((g2,)), dma((g1,)), dma((g1,)),
    ]
    whole = pl.BlockSpec(memory_space=pltpu.VMEM)
    call = pl.pallas_call(
        body,
        out_shape=(
            jax.ShapeDtypeStruct((4, 64, 64), BF16),
            jax.ShapeDtypeStruct((4, 32, 512), BF16),
            jax.ShapeDtypeStruct((27, 32, 32), F32),
            jax.ShapeDtypeStruct((27, 32, 32), F32),
            jax.ShapeDtypeStruct((8, 32, 64), F32),
        ),
        in_specs=[pl.BlockSpec(memory_space=pltpu.SMEM)] + [whole] * 6,
        out_specs=(whole,) * 5,
        scratch_shapes=scratch,
        compiler_params=pltpu.CompilerParams(
            collective_id=0, has_side_effects=True, vmem_limit_bytes=60 * 1024 * 1024
        ),
    )

    def on_device(features, voxel_mask, brick_cell, conv_one, conv_two, down_weight, cotangent):
        def turned(x):
            return x[::-1].transpose(0, 2, 1)

        wcat = jnp.stack([conv_one, conv_two, turned(conv_one), turned(conv_two)]).reshape(3456, 32)
        dwn = down_weight.reshape(256, 64)
        dwt = down_weight.reshape(2, 2, 2, 32, 64).transpose(0, 2, 4, 1, 3).reshape(256, 64)
        down, gf, w1, w2, wd = call(
            brick_cell, features, voxel_mask, cotangent.reshape(4, 64, 64), wcat, dwn, dwt
        )
        return down.reshape(4, 4096), gf, w1, w2, wd

    return on_device


def solution(mesh):
    rows = P(("region", "tile"), None)
    cube = P(("region", "tile"), None, None)
    in_specs = (cube, rows, P(("region", "tile")), P(), P(), P(), rows)
    out_specs = (rows, cube, P(), P(), P())
    return jax.shard_map(
        build(mesh.shape["region"], mesh.shape["tile"]),
        mesh=mesh,
        in_specs=in_specs,
        out_specs=out_specs,
        check_vma=False,
    )
```

```python
import math

import jax
import jax.numpy as jnp
from jax import lax
from jax.experimental import pallas as pl
from jax.experimental.pallas import tpu as pltpu
from jax.sharding import PartitionSpec as P

MESH = pl.DeviceIdType.MESH
F32 = jnp.float32
BF16 = jnp.bfloat16
NT = (((1,), (1,)), ((), ()))
TN = (((0,), (0,)), ((), ()))


def mm(a, b):
    return jnp.dot(a, b, preferred_element_type=F32)


def mmd(a, b, dims):
    return lax.dot_general(a, b, dims, preferred_element_type=F32)


def iota(shape, dim):
    return lax.broadcasted_iota(jnp.int32, shape, dim)


def one_hot(cond):
    return jnp.where(cond, 1.0, 0.0)


def shift_z(rows, amount):
    count = rows.shape[0]
    z = iota(rows.shape, 0) % 32
    rolled = pltpu.roll(rows, (-amount) % count, 0)
    keep = (z < 31) if amount > 0 else (z > 0)
    return jnp.where(keep, rolled, 0.0)


def put_center(fk, first_x, rows):
    n = rows.shape[0] // 32
    for k, amount in enumerate((-1, 0, 1)):
        moved = rows if amount == 0 else shift_z(rows, amount)
        fk[pl.ds(first_x, n), :, :, 256 * k : 256 * k + 256] = moved.reshape(n, 4, 8, 256).astype(BF16)


def pack_edge(rows, lane0, lanes):
    n = rows.shape[0] // 32
    cube = rows.reshape(n, 4, 8, 128)
    total = None
    for zb in range(4):
        part = cube[:, zb].reshape(n * 8, 128)
        turn = (32 * zb - lane0) % 128
        if turn:
            part = pltpu.roll(part, turn, 1)
        total = part if total is None else jnp.where(lanes // 32 == zb, part, total)
    return total


def put_edges(fk, first_x, low, high):
    n = low.shape[0] // 8
    lane = iota((n * 8, 128), 1)
    parts = []
    for zb in range(4):
        a = low if zb == 0 else pltpu.roll(low, (-32 * zb) % 128, 1)
        turn = (32 - 32 * zb) % 128
        b = high if turn == 0 else pltpu.roll(high, turn, 1)
        parts.append(jnp.where(lane < 32, a, jnp.where(lane < 64, b, 0.0)).reshape(n, 1, 8, 128))
    v = jnp.concatenate(parts, axis=1).reshape(n * 32, 128)
    first = shift_z(v, -1) + pltpu.roll(v, 64, 1)
    fk[pl.ds(first_x, n), :, :, 768:896] = first.reshape(n, 4, 8, 128).astype(BF16)
    fk[pl.ds(first_x, n), :, :, 896:1024] = shift_z(v, 1).reshape(n, 4, 8, 128).astype(BF16)


def window(fk, cells, dx):
    return jnp.concatenate(
        [fk[pl.ds(8 * (e // 4) + dx, 8), e % 4].reshape(64, 1024) for e in cells], axis=0
    )


def conv(fk, cells, t_ref, kind):
    total = None
    for dx in range(3):
        term = mm(window(fk, cells, dx), t_ref[kind, dx])
        total = term if total is None else total + term
    return total


def kernel_grad(xt, fk, cells, mscr, blocks):
    lane = iota((32, 256), 1)
    for dx in range(3):
        mscr[...] = mm(xt, window(fk, cells, dx))
        for dz in range(3):
            total = None
            for j in range(8):
                piece = mscr[32 * j : 32 * j + 32, 256 * dz : 256 * dz + 256]
                if j in (0, 7):
                    edge = mscr[32 * j : 32 * j + 32, 768:1024]
                    have = 64 * dz + (0 if j == 0 else 32)
                    want = 224 if j == 0 else 0
                    turn = (want - have) % 256
                    if turn:
                        edge = pltpu.roll(edge, turn, 1)
                    piece = jnp.where(lane // 32 == want // 32, edge, piece)
                turn = (32 - 32 * j) % 256
                if turn:
                    piece = pltpu.roll(piece, turn, 1)
                total = piece if total is None else total + piece
            blocks[3 * dx + dz] = total[:, 0:128]


def pack_blocks(blocks, dst, first):
    lane = iota((32, 128), 1)
    for g in range(7):
        value = blocks[g]
        if g < 6:
            extra = pltpu.roll(blocks[7 + g // 3], 32 * (3 - g % 3), 1)
            value = jnp.where(lane < 96, value, extra)
        dst[first + 32 * g : first + 32 * g + 32, :] = value.astype(BF16)


def tap_of(group, slot):
    block, dy = (group, slot) if slot < 3 else (7 + group // 3, group % 3)
    return 9 * (block // 3) + 3 * dy + block % 3


def finish(pw, pd, gf, down, o_down, o_gf, o_w1, o_w2, o_wd):
    for g in range(7):
        one = pw[32 * g : 32 * g + 32, :].astype(F32).T
        two = pw[224 + 32 * g : 224 + 32 * g + 32, :].astype(F32)
        for slot in range(4 if g < 6 else 3):
            k = tap_of(g, slot)
            o_w1[k] = one[32 * slot : 32 * slot + 32, :]
            o_w2[26 - k] = two[:, 32 * slot : 32 * slot + 32]
    for a in range(2):
        for b in range(2):
            for d in range(2):
                o_wd[4 * a + 2 * b + d] = pd[64 * a + 32 * b : 64 * a + 32 * b + 32, 64 * d : 64 * d + 64]
    o_gf[...] = gf[...]
    o_down[...] = down[...]


def build(n_r, n_t):
    inner = min(16, n_t)
    outer = n_t // inner
    g1 = n_r * outer
    g2 = inner
    rows_w = 512 // g1
    rows_d = 128 // g1
    scale = 1.0 / math.sqrt(4 * n_r * n_t * 512.0)

    def body(
        bc, feat_h, vmask_h, cot_h, one_h, two_h, dw_h,
        o_pw, o_pd, o_gf, o_down,
        feat, vmask, cot, wraw, dw,
        tmats, wtile, wdn, wback, pick, slots, crow, cots, inps, masks, back,
        fki, fkg, fkh, fkf, mscr, blocks, blocks2,
        sx, sy, sc, rx, ry, rc,
        pw, p1, q1, p2, q2, p3, q3, pd, d1, e1, d2, e2, d3, e3,
        ins, hs, hr, w1s, w1r, w2s, w2r, w3s, w3r, d1s, d1r, d2s, d2r, d3s, d3r,
    ):
        loads = [
            pltpu.make_async_copy(src, dst, ins.at[k])
            for k, (src, dst) in enumerate(
                [(feat_h, feat), (vmask_h, vmask), (cot_h, cot), (dw_h, dw), (one_h, wraw.at[0]), (two_h, wraw.at[1])]
            )
        ]
        for c in loads:
            c.start()
        r = lax.axis_index("region")
        t = lax.axis_index("tile")
        y = t // inner
        u = t % inner
        m = r * outer + y

        def peer1(k):
            return (k // outer, (k % outer) * inner + u)

        def peer2(k):
            return (r, y * inner + k)

        near = [(dr, dt) for dr in (-1, 0, 1) for dt in (-1, 0, 1) if (dr, dt) != (0, 0)]

        def neighbour(dr, dt):
            return ((r + dr + n_r) % n_r, (t + dt + n_t) % n_t)

        barrier = pltpu.get_barrier_semaphore()
        for dr, dt in near:
            pl.semaphore_signal(barrier, inc=1, device_id=neighbour(dr, dt), device_id_type=MESH)

        def greet1(k, carry):
            pl.semaphore_signal(barrier, inc=1, device_id=peer1((m + k) % g1), device_id_type=MESH)
            return carry

        def greet2(k, carry):
            pl.semaphore_signal(barrier, inc=1, device_id=peer2((u + k) % g2), device_id_type=MESH)
            return carry

        lax.fori_loop(1, g1, greet1, 0)
        lax.fori_loop(1, g2, greet2, 0)

        cells = [jnp.maximum(bc[s], 0) for s in range(4)]
        lives = [jnp.where(bc[s] >= 0, 1.0, 0.0) for s in range(4)]
        owners = []
        for e in range(8):
            owner = jnp.int32(4)
            for s in range(4):
                owner = jnp.where(bc[s] == e, jnp.int32(s), owner)
            owners.append(owner)

        v = iota((64, 512), 1)
        w = iota((64, 512), 0)
        pick[...] = one_hot((v // 64 == w // 8) & (v % 8 == w % 8)).astype(BF16)
        jmask = one_hot(iota((256, 512), 1) // 8 % 8 == iota((256, 512), 0) // 32).astype(BF16)
        jcols = one_hot(iota((512, 256), 0) // 8 % 8 == iota((512, 256), 1) // 32).astype(BF16)
        cv = iota((32, 64), 1)
        cw = iota((32, 64), 0)
        up = one_hot((cv // 16 == cw // 8) & (cv % 4 == cw % 8 // 2)).astype(BF16)
        even = one_hot((cv // 16 == cw // 8) & (2 * (cv % 4) == cw % 8)).astype(BF16)
        ymask = one_hot(iota((256, 64), 1) // 4 % 4 == iota((256, 64), 0) // 64).astype(BF16)
        slots[4] = jnp.zeros((64, 256), F32)

        def halo(phase, field):
            plan = [
                (sx.at[phase, field, 0], rx.at[phase, field, 1], (-1, 0)),
                (sx.at[phase, field, 1], rx.at[phase, field, 0], (1, 0)),
                (sy.at[phase, field, 0], ry.at[phase, field, 1], (0, -1)),
                (sy.at[phase, field, 1], ry.at[phase, field, 0], (0, 1)),
                (sc.at[phase, field, 0], rc.at[phase, field, 3], (-1, -1)),
                (sc.at[phase, field, 1], rc.at[phase, field, 2], (-1, 1)),
                (sc.at[phase, field, 2], rc.at[phase, field, 1], (1, -1)),
                (sc.at[phase, field, 3], rc.at[phase, field, 0], (1, 1)),
            ]
            copies = [
                pltpu.make_async_remote_copy(
                    src_ref=src,
                    dst_ref=dst,
                    send_sem=hs.at[phase, field, k],
                    recv_sem=hr.at[phase, field, k],
                    device_id=neighbour(dr, dt),
                    device_id_type=MESH,
                )
                for k, (src, dst, (dr, dt)) in enumerate(plan)
            ]
            return copies

        def place(phase, field, fk):
            lanes = iota((64, 128), 1)
            for part in range(2):
                rows = jnp.concatenate(
                    [slots[owners[4 * part + zb]].reshape(8, 1, 8, 256) for zb in range(4)], axis=1
                ).reshape(256, 256)
                put_center(fk, 1 + 8 * part, rows)
                low = pack_edge(rows[:, 0:128], 0, lanes)
                high = pack_edge(rows[:, 128:256], 96, lanes)
                sy[phase, field, 0, 64 * part : 64 * part + 64, :] = low.astype(BF16)
                sy[phase, field, 1, 64 * part : 64 * part + 64, :] = high.astype(BF16)
                a = 224 * part
                b = 56 * part
                sx[phase, field, part] = rows[a : a + 32].astype(BF16)
                sc[phase, field, 2 * part] = low[b : b + 8].astype(BF16)
                sc[phase, field, 2 * part + 1] = high[b : b + 8].astype(BF16)

        has = [
            jnp.where(r > 0, 1.0, 0.0),
            jnp.where(r < n_r - 1, 1.0, 0.0),
            jnp.where(t > 0, 1.0, 0.0),
            jnp.where(t < n_t - 1, 1.0, 0.0),
        ]

        def put_halo(phase, field, fk):
            put_center(fk, 0, rx[phase, field, 0].astype(F32) * has[0])
            put_center(fk, 17, rx[phase, field, 1].astype(F32) * has[1])
            for part in range(2):
                rows = slice(64 * part, 64 * part + 64)
                put_edges(
                    fk,
                    1 + 8 * part,
                    ry[phase, field, 0, rows].astype(F32) * has[2],
                    ry[phase, field, 1, rows].astype(F32) * has[3],
                )
            for side in range(2):
                put_edges(
                    fk,
                    17 * side,
                    rc[phase, field, 2 * side].astype(F32) * (has[side] * has[2]),
                    rc[phase, field, 2 * side + 1].astype(F32) * (has[side] * has[3]),
                )

        loads[0].wait()
        loads[1].wait()
        for s in range(4):
            seen = jnp.broadcast_to((vmask[s : s + 1, :].astype(F32) * lives[s]), (64, 512)).astype(BF16)
            masks[64 * s : 64 * s + 64, :] = mm(pick[...] * seen, jcols)
            tall = jnp.concatenate([feat[s] * seen[0:32]] * 8, axis=0) * jmask
            got = mmd(pick[...], tall, NT)
            inps[64 * s : 64 * s + 64, :] = got
            slots[s] = got
        place(0, 0, fki)
        pl.semaphore_wait(barrier, 8 + (g1 - 1) + (g2 - 1))
        first = halo(0, 0)
        for c in first:
            c.start()

        loads[2].wait()
        loads[3].wait()
        dwide = dw[...].reshape(256, 64).astype(F32)
        dtile = jnp.concatenate([dwide, dwide], axis=1)
        lane64 = iota((32, 128), 1) // 64
        for a in range(2):
            for b in range(2):
                for d in range(2):
                    k = 4 * a + 2 * b + d
                    block = dtile[32 * k : 32 * k + 32]
                    for y4 in range(4):
                        row = 256 * a + 32 * (2 * y4 + b)
                        for half in range(2):
                            col = 256 * d + 128 * half
                            if y4 // 2 == half:
                                value = jnp.where(lane64 == y4 % 2, block, 0.0).astype(BF16)
                            else:
                                value = jnp.zeros((32, 128), BF16)
                            wdn[row : row + 32, col : col + 128] = value
        lane32 = iota((64, 128), 1)
        for a in range(2):
            turned = dtile[128 * a : 128 * a + 128, :].T[0:64]
            for d in range(2):
                low = turned if d == 0 else pltpu.roll(turned, 96, 1)
                high = pltpu.roll(turned, 96 - 32 * d, 1)
                pair = jnp.where(lane32 < 32, low, jnp.where(lane32 < 64, high, 0.0))
                pair = pair + pltpu.roll(pair, 64, 1)
                for y4 in range(4):
                    for half in range(2):
                        col = 512 * a + 256 * d + 128 * half
                        if y4 // 2 == half:
                            value = jnp.where(lane32 // 64 == y4 % 2, pair, 0.0).astype(BF16)
                        else:
                            value = jnp.zeros((64, 128), BF16)
                        wback[64 * y4 : 64 * y4 + 64, col : col + 128] = value

        for k in range(32):
            part = cot[:, 128 * k : 128 * k + 128].astype(F32)
            cots[pl.ds(16 * k, 4), :] = part
            cots[pl.ds(16 * k + 8, 4), :] = pltpu.roll(part, 64, 1)
        for s in range(4):
            native = cots[pl.ds(s, 64, stride=8), :][:, 0:64].astype(BF16)
            tall = jnp.concatenate([native] * 4, axis=0) * ymask
            crow[32 * s : 32 * s + 32, :] = mmd(up, tall, NT)
        crow_b = crow[...].astype(BF16)
        odd = iota((128, 256), 0) % 2 == 1
        for a in range(2):
            back[:, a] = jnp.where(
                odd,
                mm(crow_b, wback[:, 512 * a + 256 : 512 * a + 512]),
                mm(crow_b, wback[:, 512 * a : 512 * a + 256]),
            ).reshape(16, 8, 256)
        for s in range(4):
            rows = back[4 * s : 4 * s + 4].reshape(64, 256) * masks[64 * s : 64 * s + 64, :]
            slots[s] = rows.astype(BF16).astype(F32)
        place(0, 1, fkg)
        second = halo(0, 1)
        for c in second:
            c.start()

        loads[4].wait()
        loads[5].wait()
        for c in range(2):
            flat = wraw[c].reshape(864, 32).astype(F32)
            wtile[c, 0:864, :] = jnp.concatenate([flat] * 4, axis=1).astype(BF16)
            wtile[c, 864:896, :] = jnp.zeros((32, 128), BF16)
        lane = iota((32, 128), 1)
        for c in range(2):
            for g in range(7):
                turned = wtile[c, 128 * g : 128 * g + 128, :].T[0:32].astype(F32)
                for k in range(4 if g < 6 else 3):
                    piece = jnp.where(lane // 32 == k, turned, 0.0)
                    piece = piece + pltpu.roll(piece, 32, 1)
                    piece = piece + pltpu.roll(piece, 64, 1)
                    at = 32 * (26 - 4 * g - k)
                    wtile[2 + c, at : at + 32, :] = piece.astype(BF16)
        quarter = [one_hot(lane // 32 == k).astype(BF16) for k in range(4)]
        nothing = jnp.zeros((32, 128), BF16)

        def band(kind, carry):
            for dx in range(3):
                for dz in range(3):
                    low, mid, high = (
                        wtile[kind, 32 * (9 * dx + 3 * dy + dz) : 32 * (9 * dx + 3 * dy + dz) + 32, :]
                        for dy in range(3)
                    )
                    for j in range(8):
                        for half in range(2):
                            value = None
                            for jo, tap in ((j - 1, high), (j, mid), (j + 1, low)):
                                if 4 * half <= jo < 4 * half + 4:
                                    term = tap * quarter[jo - 4 * half]
                                    value = term if value is None else value + term
                            at = 256 * dz + 32 * j
                            tmats[kind, dx, at : at + 32, 128 * half : 128 * half + 128] = (
                                nothing if value is None else value
                            )
                    at = 768 + 64 * dz
                    tmats[kind, dx, at : at + 32, 0:128] = low * quarter[0]
                    tmats[kind, dx, at : at + 32, 128:256] = nothing
                    tmats[kind, dx, at + 32 : at + 64, 0:128] = nothing
                    tmats[kind, dx, at + 32 : at + 64, 128:256] = high * quarter[3]
                for at in (960, 992):
                    tmats[kind, dx, at : at + 32, 0:128] = nothing
                    tmats[kind, dx, at : at + 32, 128:256] = nothing
            return carry

        lax.fori_loop(0, 4, band, 0)

        for c in first:
            c.wait_recv()
        put_halo(0, 0, fki)
        before = conv(fki, cells, tmats, 0) * masks[...]
        sig = 1.0 / (1.0 + jnp.exp(-before))
        hidden = (before / (1.0 + jnp.exp(-before))).astype(BF16)
        hidden_t = hidden.T
        slope = sig * (1.0 + before * (1.0 - sig)) * masks[...]
        slots[0:4] = hidden.astype(F32).reshape(4, 64, 256)
        place(1, 0, fkh)
        third = halo(1, 0)
        for c in third:
            c.start()

        for c in second:
            c.wait_recv()
        put_halo(0, 1, fkg)
        grad = (conv(fkg, cells, tmats, 3) * slope).astype(BF16)
        slots[0:4] = grad.astype(F32).reshape(4, 64, 256)
        place(1, 1, fkf)
        fourth = halo(1, 1)
        for c in fourth:
            c.start()

        kernel_grad(grad.T, fki, cells, mscr, blocks)
        pack_blocks(blocks, pw, 0)
        kernel_grad(hidden_t, fkg, cells, mscr, blocks2)
        pack_blocks(blocks2, pw, 224)
        pw[448:480, :] = jnp.zeros((32, 128), BF16)
        pw[480:512, :] = jnp.zeros((32, 128), BF16)
        for k in range(g1):
            p1[k] = pw[rows_w * k : rows_w * k + rows_w, :]
        q1[m] = p1[m]

        def start_all(src, dst, mine, count, peer, send, recv, by_peer):
            def go(k, carry):
                other = (mine + k) % count
                pltpu.make_async_remote_copy(
                    src_ref=src.at[other] if by_peer else src,
                    dst_ref=dst.at[mine],
                    send_sem=send.at[k],
                    recv_sem=recv.at[k],
                    device_id=peer(other),
                    device_id_type=MESH,
                ).start()
                return carry

            lax.fori_loop(1, count, go, 0)

        def wait_all(src, dst, mine, count, peer, send, recv, by_peer):
            def go(k, carry):
                other = (mine + count - k) % count
                c = pltpu.make_async_remote_copy(
                    src_ref=src.at[other] if by_peer else src,
                    dst_ref=dst.at[other],
                    send_sem=send.at[k],
                    recv_sem=recv.at[k],
                    device_id=peer(other),
                    device_id_type=MESH,
                )
                c.wait_recv()
                c.wait_send()
                return carry

            lax.fori_loop(1, count, go, 0)

        plan_w1 = (p1, q1, m, g1, peer1, w1s, w1r, True)
        plan_w2 = (p2, q2, u, g2, peer2, w2s, w2r, False)
        plan_w3 = (p3, q3, m, g1, peer1, w3s, w3r, False)
        plan_d1 = (d1, e1, m, g1, peer1, d1s, d1r, True)
        plan_d2 = (d2, e2, u, g2, peer2, d2s, d2r, False)
        plan_d3 = (d3, e3, m, g1, peer1, d3s, d3r, False)

        def added(ref, count):
            total = ref[0].astype(F32)
            for k in range(1, count):
                total = total + ref[k].astype(F32)
            return total

        start_all(*plan_w1)

        for c in third:
            c.wait_recv()
        put_halo(1, 0, fkh)
        summed = (inps[...] + conv(fkh, cells, tmats, 1) * masks[...]).reshape(16, 2, 8, 256)
        lhs = jnp.concatenate(
            [summed[:, 0].reshape(128, 256), summed[:, 1].reshape(128, 256)], axis=1
        ).astype(BF16)

        crow_f = crow[...]
        rhs = jnp.concatenate(
            [jnp.where(odd, 0.0, crow_f).astype(BF16), jnp.where(odd, crow_f, 0.0).astype(BF16)], axis=1
        )
        low64 = iota((64, 128), 1) < 64
        for a in range(2):
            mscr[:, 0:512] = mm(lhs[:, 256 * a : 256 * a + 256].T, rhs)
            halves = []
            for d in range(2):
                c0 = 256 * d
                even_part = mscr[0:64, c0 : c0 + 128] + mscr[128:192, c0 + 128 : c0 + 256]
                odd_part = mscr[64:128, c0 : c0 + 128] + mscr[192:256, c0 + 128 : c0 + 256]
                if d == 0:
                    halves.append(even_part + pltpu.roll(odd_part, 64, 1))
                else:
                    halves.append(pltpu.roll(even_part, 64, 1) + odd_part)
            pd[64 * a : 64 * a + 64, :] = jnp.where(low64, halves[0], halves[1])
        for k in range(g1):
            d1[k] = pd[rows_d * k : rows_d * k + rows_d, :]
        e1[m] = d1[m]
        start_all(*plan_d1)

        rows = mm(lhs, wdn[:, 0:256]) + pltpu.roll(mm(lhs, wdn[:, 256:512]), 127, 0)
        rows = rows.astype(BF16)
        for s in range(4):
            wide = mmd(rows[32 * s : 32 * s + 32, :], even, TN)
            total = None
            for y4 in range(4):
                part = jnp.where(iota((64, 64), 1) // 4 % 4 == y4, wide[64 * y4 : 64 * y4 + 64], 0.0)
                total = part if total is None else total + part
            cots[pl.ds(s, 64, stride=8), :] = jnp.concatenate([total, total], axis=1)
        low4 = iota((4, 128), 1) < 64
        for k in range(32):
            o_down[:, 128 * k : 128 * k + 128] = jnp.where(
                low4, cots[pl.ds(16 * k, 4), :], cots[pl.ds(16 * k + 8, 4), :]
            ).astype(BF16)

        wait_all(*plan_w1)
        p2[...] = added(q1, g1).astype(BF16)
        q2[u] = p2[...]
        start_all(*plan_w2)

        for c in fourth:
            c.wait_recv()
        put_halo(1, 1, fkf)
        value = (back[...].reshape(256, 256) + conv(fkf, cells, tmats, 2)) * masks[...]
        value = value.astype(BF16)

        wait_all(*plan_d1)
        d2[...] = added(e1, g1)
        e2[u] = d2[...]
        start_all(*plan_d2)

        jl512 = iota((32, 512), 1) // 8 % 8
        for s in range(4):
            wide = mmd(value[64 * s : 64 * s + 64, :], pick[...], TN)
            total = None
            for j in range(8):
                part = jnp.where(jl512 == j, wide[32 * j : 32 * j + 32], 0.0)
                total = part if total is None else total + part
            o_gf[s] = total.astype(BF16)

        wait_all(*plan_w2)
        p3[...] = (added(q2, g2) * scale).astype(BF16)
        q3[m] = p3[...]
        start_all(*plan_w3)
        wait_all(*plan_d2)
        d3[...] = added(e2, g2) * scale
        e3[m] = d3[...]
        start_all(*plan_d3)

        wait_all(*plan_w3)
        for k in range(g1):
            o_pw[rows_w * k : rows_w * k + rows_w, :] = q3[k]
        wait_all(*plan_d3)
        for k in range(g1):
            o_pd[rows_d * k : rows_d * k + rows_d, :] = e3[k]
        for c in first + second + third + fourth:
            c.wait_send()

    def vm(shape, dtype=F32):
        return pltpu.VMEM(shape, dtype)

    dma = pltpu.SemaphoreType.DMA
    field = vm((18, 4, 8, 1024), BF16)
    scratch = [
        vm((4, 32, 512), BF16), vm((4, 512), jnp.int32), vm((4, 4096), BF16), vm((2, 27, 32, 32), BF16), vm((8, 32, 64), BF16),
        vm((4, 3, 1024, 256), BF16), vm((4, 896, 128), BF16), vm((512, 512), BF16), vm((256, 1024), BF16),
        vm((64, 512), BF16), vm((5, 64, 256)), vm((128, 256)), vm((512, 128)), vm((256, 256)), vm((256, 256)), vm((16, 2, 8, 256)),
        field, field, field, field, vm((256, 1024)), vm((9, 32, 128)), vm((9, 32, 128)),
        vm((2, 2, 2, 32, 256), BF16), vm((2, 2, 2, 128, 128), BF16), vm((2, 2, 4, 8, 128), BF16),
        vm((2, 2, 2, 32, 256), BF16), vm((2, 2, 2, 128, 128), BF16), vm((2, 2, 4, 8, 128), BF16),
        vm((512, 128), BF16), vm((g1, rows_w, 128), BF16), vm((g1, rows_w, 128), BF16),
        vm((rows_w, 128), BF16), vm((g2, rows_w, 128), BF16), vm((rows_w, 128), BF16), vm((g1, rows_w, 128), BF16),
        vm((128, 128)), vm((g1, rows_d, 128)), vm((g1, rows_d, 128)),
        vm((rows_d, 128)), vm((g2, rows_d, 128)), vm((rows_d, 128)), vm((g1, rows_d, 128)),
        dma((6,)), dma((2, 2, 8)), dma((2, 2, 8)),
        dma((g1,)), dma((g1,)), dma((g2,)), dma((g2,)), dma((g1,)), dma((g1,)),
        dma((g1,)), dma((g1,)), dma((g2,)), dma((g2,)), dma((g1,)), dma((g1,)),
    ]
    whole = pl.BlockSpec(memory_space=pltpu.VMEM)
    far = pl.BlockSpec(memory_space=pltpu.HBM)
    step = pl.pallas_call(
        body,
        out_shape=(
            jax.ShapeDtypeStruct((512, 128), BF16),
            jax.ShapeDtypeStruct((128, 128), F32),
            jax.ShapeDtypeStruct((4, 32, 512), BF16),
            jax.ShapeDtypeStruct((4, 4096), BF16),
        ),
        in_specs=[pl.BlockSpec(memory_space=pltpu.SMEM)] + [far] * 6,
        out_specs=(whole,) * 4,
        scratch_shapes=scratch,
        compiler_params=pltpu.CompilerParams(
            collective_id=0, has_side_effects=True, vmem_limit_bytes=32 * 1024 * 1024
        ),
    )
    last = pl.pallas_call(
        finish,
        out_shape=(
            jax.ShapeDtypeStruct((4, 4096), BF16),
            jax.ShapeDtypeStruct((4, 32, 512), BF16),
            jax.ShapeDtypeStruct((27, 32, 32), F32),
            jax.ShapeDtypeStruct((27, 32, 32), F32),
            jax.ShapeDtypeStruct((8, 32, 64), F32),
        ),
        in_specs=[whole] * 4,
        out_specs=(whole,) * 5,
        compiler_params=pltpu.CompilerParams(vmem_limit_bytes=8 * 1024 * 1024),
    )

    def on_device(features, voxel_mask, brick_cell, conv_one, conv_two, down_weight, cotangent):
        pw, pd, gf, down = step(
            *[
                pltpu.with_memory_space_constraint(x, pltpu.HBM)
                for x in (brick_cell, features, voxel_mask, cotangent, conv_one, conv_two, down_weight)
            ]
        )
        return last(pw, pd, gf, down)

    return on_device


def solution(mesh):
    rows = P(("region", "tile"), None)
    cube = P(("region", "tile"), None, None)
    in_specs = (cube, rows, P(("region", "tile")), P(), P(), P(), rows)
    out_specs = (rows, cube, P(), P(), P())
    return jax.shard_map(
        build(mesh.shape["region"], mesh.shape["tile"]),
        mesh=mesh,
        in_specs=in_specs,
        out_specs=out_specs,
        check_vma=False,
    )
```

```python
import math

import jax
import jax.numpy as jnp
from jax import lax
from jax.experimental import pallas as pl
from jax.experimental.pallas import tpu as pltpu
from jax.sharding import PartitionSpec as P

MESH = pl.DeviceIdType.MESH
F32 = jnp.float32
BF16 = jnp.bfloat16
NT = (((1,), (1,)), ((), ()))
TN = (((0,), (0,)), ((), ()))


def mm(a, b):
    return jnp.dot(a, b, preferred_element_type=F32)


def mmd(a, b, dims):
    return lax.dot_general(a, b, dims, preferred_element_type=F32)


def iota(shape, dim):
    return lax.broadcasted_iota(jnp.int32, shape, dim)


def one_hot(cond):
    return jnp.where(cond, 1.0, 0.0)


def put(fk, zb, first_x, value, lanes):
    n = value.shape[0] // 8
    for xb in range(2):
        base = 8 * xb
        for a, b in ((base, base + 1), (base + 1, base + 9), (base + 9, base + 10)):
            a, b = max(a, first_x), min(b, first_x + n)
            if a < b:
                part = value[8 * (a - first_x) : 8 * (b - first_x)]
                fk[4 * xb + zb, 8 * (a - base) + 8 : 8 * (b - base) + 8, lanes] = part.astype(BF16)


def put_center(fk, first_x, rows):
    n = rows.shape[0] // 32
    cube = rows.reshape(4 * n, 8, 256)
    down = pltpu.roll(cube, 1, 1).reshape(n, 4, 8, 256)
    up = pltpu.roll(cube, 7, 1).reshape(n, 4, 8, 256)
    cube = cube.reshape(n, 4, 8, 256)
    row = iota((n, 8, 256), 1)
    for zb in range(4):
        below = jnp.where(row > 0, down[:, zb], down[:, zb - 1] if zb > 0 else 0.0)
        above = jnp.where(row < 7, up[:, zb], up[:, zb + 1] if zb < 3 else 0.0)
        for k, part in enumerate((below, cube[:, zb], above)):
            flat = part.reshape(8 * n, 256)
            put(fk, zb, first_x, flat[:, 0:128], slice(128 * k, 128 * k + 128))
            put(fk, zb, first_x, flat[:, 128:256], slice(512 + 128 * k, 640 + 128 * k))


def pack_edge(rows, lane0, lanes):
    n = rows.shape[0] // 32
    cube = rows.reshape(n, 4, 8, 128)
    total = None
    for zb in range(4):
        part = cube[:, zb].reshape(n * 8, 128)
        turn = (32 * zb - lane0) % 128
        if turn:
            part = pltpu.roll(part, turn, 1)
        total = part if total is None else jnp.where(lanes // 32 == zb, part, total)
    return total


def put_edges(fk, first_x, side, packed):
    n = packed.shape[0] // 8
    lane = iota((n * 8, 128), 1)
    row = iota((n * 8, 128), 0) % 8
    cube = packed.reshape(n, 8, 128)
    down = pltpu.roll(cube, 1, 1).reshape(n * 8, 128)
    down = jnp.where(row > 0, down, jnp.where(lane >= 32, pltpu.roll(down, 32, 1), 0.0))
    up = pltpu.roll(cube, 7, 1).reshape(n * 8, 128)
    up = jnp.where(row < 7, up, jnp.where(lane < 96, pltpu.roll(up, 96, 1), 0.0))
    for zb in range(4):
        value = 0.0
        for k, part in ((2, up), (1, packed), (0, down)):
            turn = (32 * k - 32 * zb) % 128
            value = jnp.where(lane < 32 * k + 32, pltpu.roll(part, turn, 1) if turn else part, value)
        at = 512 * side + 384
        put(fk, zb, first_x, value, slice(at, at + 128))


def window(fk, cells, dx):
    return jnp.concatenate([fk[e, 8 * dx + 8 : 8 * dx + 72, :] for e in cells], axis=0)


def conv(fk, cells, t_ref, kind):
    total = None
    for dx in range(3):
        term = mm(window(fk, cells, dx), t_ref[kind, dx])
        total = term if total is None else total + term
    return total


def kernel_grad(xt, fk, cells, blocks):
    lane = iota((32, 128), 1)
    for dx in range(3):
        near = window(fk, cells, dx)
        low = mm(xt[0:160], near[:, 0:512])
        high = mm(xt[96:256], near[:, 512:1024])
        for dz in range(3):
            lo = [low[32 * j : 32 * j + 32, 128 * dz : 128 * dz + 128] for j in range(5)]
            hi = [high[32 * j : 32 * j + 32, 128 * dz : 128 * dz + 128] for j in range(5)]
            still = lo[1] + hi[2]
            back = lo[2] + hi[3]
            half = jnp.where(lane >= 64, lo[3] + hi[4], jnp.where(lane < 32, hi[0], 0.0))
            ahead = jnp.where(lane >= 96, lo[4], jnp.where(lane < 64, hi[1] + lo[0], 0.0))
            mine = lane // 32 == dz
            first = jnp.where(mine, low[0:32, 384:512], 0.0)
            last = jnp.where(mine, high[128:160, 384:512], 0.0)
            if dz == 0:
                still, half = still + first, half + last
            elif dz == 1:
                back, ahead = back + first, ahead + last
            else:
                half, still = half + first, still + last
            blocks[3 * dx + dz] = (
                still + pltpu.roll(back, 96, 1) + pltpu.roll(half, 64, 1) + pltpu.roll(ahead, 32, 1)
            )


def pack_blocks(blocks, dst, first):
    lane = iota((32, 128), 1)
    for g in range(7):
        value = blocks[g]
        if g < 6:
            extra = pltpu.roll(blocks[7 + g // 3], 32 * (3 - g % 3), 1)
            value = jnp.where(lane < 96, value, extra)
        dst[first + 32 * g : first + 32 * g + 32, :] = value.astype(BF16)


def tap_of(group, slot):
    block, dy = (group, slot) if slot < 3 else (7 + group // 3, group % 3)
    return 9 * (block // 3) + 3 * dy + block % 3


def finish(pw, pd, gf, down, o_down, o_gf, o_w1, o_w2, o_wd):
    for g in range(7):
        one = pw[32 * g : 32 * g + 32, :].astype(F32).T
        two = pw[224 + 32 * g : 224 + 32 * g + 32, :].astype(F32)
        for slot in range(4 if g < 6 else 3):
            k = tap_of(g, slot)
            o_w1[k] = one[32 * slot : 32 * slot + 32, :]
            o_w2[26 - k] = two[:, 32 * slot : 32 * slot + 32]
    for a in range(2):
        for b in range(2):
            for d in range(2):
                o_wd[4 * a + 2 * b + d] = pd[64 * a + 32 * b : 64 * a + 32 * b + 32, 64 * d : 64 * d + 64]
    o_gf[...] = gf[...]
    o_down[...] = down[...]


def build(n_r, n_t):
    inner = min(16, n_t)
    outer = n_t // inner
    g1 = n_r * outer
    g2 = inner
    rows_w = 512 // g1
    rows_d = 128 // g1
    scale = 1.0 / math.sqrt(4 * n_r * n_t * 512.0)

    def body(
        bc, feat_h, vmask_h, cot_h, one_h, two_h, dw_h,
        o_pw, o_pd, o_gf, o_down,
        feat, vmask, cot, wraw, dw,
        tmats, wtile, wdn, wback, pick, slots, crow, cots, inps, masks, back,
        fki, fkg, fkh, fkf, mscr, blocks, blocks2,
        sbuf, rbuf,
        pw, p1, q1, p2, q2, p3, q3, pd, d1, e1, d2, e2, d3, e3,
        ins, hs, hr, w1s, w1r, w2s, w2r, w3s, w3r, d1s, d1r, d2s, d2r, d3s, d3r,
    ):
        loads = [
            pltpu.make_async_copy(src, dst, ins.at[k])
            for k, (src, dst) in enumerate(
                [(feat_h, feat), (vmask_h, vmask), (cot_h, cot), (dw_h, dw), (one_h, wraw.at[0]), (two_h, wraw.at[1])]
            )
        ]
        for c in loads:
            c.start()
        r = lax.axis_index("region")
        t = lax.axis_index("tile")
        y = t // inner
        u = t % inner
        m = r * outer + y

        def peer1(k):
            return (k // outer, (k % outer) * inner + u)

        def peer2(k):
            return (r, y * inner + k)

        near = [(dr, dt) for dr in (-1, 0, 1) for dt in (-1, 0, 1) if (dr, dt) != (0, 0)]

        def neighbour(dr, dt):
            return ((r + dr + n_r) % n_r, (t + dt + n_t) % n_t)

        barrier = pltpu.get_barrier_semaphore()
        for dr, dt in near:
            pl.semaphore_signal(barrier, inc=1, device_id=neighbour(dr, dt), device_id_type=MESH)

        def greet1(k, carry):
            pl.semaphore_signal(barrier, inc=1, device_id=peer1((m + k) % g1), device_id_type=MESH)
            return carry

        def greet2(k, carry):
            pl.semaphore_signal(barrier, inc=1, device_id=peer2((u + k) % g2), device_id_type=MESH)
            return carry

        lax.fori_loop(1, g1, greet1, 0)
        lax.fori_loop(1, g2, greet2, 0)

        cells = [jnp.maximum(bc[s], 0) for s in range(4)]
        lives = [jnp.where(bc[s] >= 0, 1.0, 0.0) for s in range(4)]
        owners = []
        for e in range(8):
            owner = jnp.int32(4)
            for s in range(4):
                owner = jnp.where(bc[s] == e, jnp.int32(s), owner)
            owners.append(owner)

        nothing = jnp.zeros((32, 128), BF16)
        for c in range(2):
            wtile[c, 864:896, :] = nothing
        for kind in range(4):
            for dx in range(3):
                for at in range(0, 1024, 32):
                    high_row = at >= 512
                    inner_row = at % 512 < 384
                    j = at % 128 // 32 + 4 * high_row
                    for half in range(2):
                        pad = at % 512 == 480
                        full = 4 * half - 1 <= j <= 4 * half + 4 if inner_row else half == high_row
                        if pad or not full:
                            tmats[kind, dx, at : at + 32, 128 * half : 128 * half + 128] = nothing

        v = iota((64, 512), 1)
        w = iota((64, 512), 0)
        pick[...] = one_hot((v // 64 == w // 8) & (v % 8 == w % 8)).astype(BF16)
        jlane = iota((32, 128), 1) // 8 % 8
        jmask = [jnp.concatenate([one_hot(jlane == j).astype(BF16)] * 4, axis=1) for j in range(8)]
        jcols = one_hot(iota((64, 256), 0) // 8 == iota((64, 256), 1) // 32).astype(BF16)
        jcols = jnp.concatenate([jcols] * 8, axis=0)
        cv = iota((32, 64), 1)
        cw = iota((32, 64), 0)
        up = one_hot((cv // 16 == cw // 8) & (cv % 4 == cw % 8 // 2)).astype(BF16)
        even = one_hot((cv // 16 == cw // 8) & (2 * (cv % 4) == cw % 8)).astype(BF16)
        ymask = one_hot(iota((256, 64), 1) // 4 % 4 == iota((256, 64), 0) // 64).astype(BF16)
        slots[4] = jnp.zeros((64, 256), F32)

        def halo(phase, field):
            plan = [
                (256, 320, 64, (-1, 0)),
                (320, 256, 64, (1, 0)),
                (0, 128, 128, (0, -1)),
                (128, 0, 128, (0, 1)),
                (384, 408, 8, (-1, -1)),
                (392, 400, 8, (-1, 1)),
                (400, 392, 8, (1, -1)),
                (408, 384, 8, (1, 1)),
            ]
            copies = [
                pltpu.make_async_remote_copy(
                    src_ref=sbuf.at[phase, field, src : src + size],
                    dst_ref=rbuf.at[phase, field, dst : dst + size],
                    send_sem=hs.at[phase, field],
                    recv_sem=hr.at[phase, field],
                    device_id=neighbour(dr, dt),
                    device_id_type=MESH,
                )
                for src, dst, size, (dr, dt) in plan
            ]
            for c in copies:
                c.start()
            return pltpu.make_async_remote_copy(
                src_ref=sbuf.at[phase, field],
                dst_ref=rbuf.at[phase, field],
                send_sem=hs.at[phase, field],
                recv_sem=hr.at[phase, field],
                device_id=neighbour(0, 1),
                device_id_type=MESH,
            )

        def place(phase, field, fk):
            lanes = iota((64, 128), 1)
            for part in range(2):
                rows = jnp.concatenate(
                    [slots[owners[4 * part + zb]].reshape(8, 1, 8, 256) for zb in range(4)], axis=1
                ).reshape(256, 256)
                put_center(fk, 1 + 8 * part, rows)
                low = pack_edge(rows[:, 0:128], 0, lanes)
                high = pack_edge(rows[:, 128:256], 96, lanes)
                sbuf[phase, field, 64 * part : 64 * part + 64, :] = low.astype(BF16)
                sbuf[phase, field, 128 + 64 * part : 192 + 64 * part, :] = high.astype(BF16)
                a = 224 * part
                b = 56 * part
                x = 256 + 64 * part
                sbuf[phase, field, x : x + 32, :] = rows[a : a + 32, 0:128].astype(BF16)
                sbuf[phase, field, x + 32 : x + 64, :] = rows[a : a + 32, 128:256].astype(BF16)
                x = 384 + 16 * part
                sbuf[phase, field, x : x + 8, :] = low[b : b + 8].astype(BF16)
                sbuf[phase, field, x + 8 : x + 16, :] = high[b : b + 8].astype(BF16)

        has = [
            jnp.where(r > 0, 1.0, 0.0),
            jnp.where(r < n_r - 1, 1.0, 0.0),
            jnp.where(t > 0, 1.0, 0.0),
            jnp.where(t < n_t - 1, 1.0, 0.0),
        ]

        def put_halo(phase, field, fk):
            for end in range(2):
                x = 256 + 64 * end
                plane = jnp.concatenate(
                    [rbuf[phase, field, x : x + 32, :], rbuf[phase, field, x + 32 : x + 64, :]], axis=1
                )
                put_center(fk, 17 * end, plane.astype(F32) * has[end])
            for side in range(2):
                face = rbuf[phase, field, 128 * side : 128 * side + 128, :]
                put_edges(fk, 1, side, face.astype(F32) * has[2 + side])
                for end in range(2):
                    x = 384 + 16 * end + 8 * side
                    packed = rbuf[phase, field, x : x + 8, :].astype(F32)
                    put_edges(fk, 17 * end, side, packed * (has[end] * has[2 + side]))

        loads[0].wait()
        loads[1].wait()
        for s in range(4):
            seen = jnp.broadcast_to((vmask[s : s + 1, :].astype(F32) * lives[s]), (64, 512)).astype(BF16)
            masks[64 * s : 64 * s + 64, :] = mm(pick[...] * seen, jcols)
            kept = feat[s] * seen[0:32]
            tall = jnp.concatenate([kept * jmask[j] for j in range(8)], axis=0)
            got = mmd(pick[...], tall, NT)
            inps[64 * s : 64 * s + 64, :] = got
            slots[s] = got
        place(0, 0, fki)
        pl.semaphore_wait(barrier, 8 + (g1 - 1) + (g2 - 1))
        first = halo(0, 0)

        loads[2].wait()
        loads[3].wait()
        dwide = dw[...].reshape(256, 64).astype(F32)
        dtile = jnp.concatenate([dwide, dwide], axis=1)
        lane64 = iota((32, 128), 1) // 64
        for a in range(2):
            for b in range(2):
                for d in range(2):
                    k = 4 * a + 2 * b + d
                    block = dtile[32 * k : 32 * k + 32]
                    for y4 in range(4):
                        row = 256 * a + 32 * (2 * y4 + b)
                        for half in range(2):
                            col = 256 * d + 128 * half
                            if y4 // 2 == half:
                                value = jnp.where(lane64 == y4 % 2, block, 0.0).astype(BF16)
                            else:
                                value = jnp.zeros((32, 128), BF16)
                            wdn[row : row + 32, col : col + 128] = value
        lane32 = iota((64, 128), 1)
        for a in range(2):
            turned = dtile[128 * a : 128 * a + 128, :].T[0:64]
            for d in range(2):
                low = turned if d == 0 else pltpu.roll(turned, 96, 1)
                high = pltpu.roll(turned, 96 - 32 * d, 1)
                pair = jnp.where(lane32 < 32, low, jnp.where(lane32 < 64, high, 0.0))
                pair = pair + pltpu.roll(pair, 64, 1)
                for y4 in range(4):
                    for half in range(2):
                        col = 512 * a + 256 * d + 128 * half
                        if y4 // 2 == half:
                            value = jnp.where(lane32 // 64 == y4 % 2, pair, 0.0).astype(BF16)
                        else:
                            value = jnp.zeros((64, 128), BF16)
                        wback[64 * y4 : 64 * y4 + 64, col : col + 128] = value

        for k in range(32):
            part = cot[:, 128 * k : 128 * k + 128].astype(F32)
            cots[pl.ds(16 * k, 4), :] = part
            cots[pl.ds(16 * k + 8, 4), :] = pltpu.roll(part, 64, 1)
        for s in range(4):
            native = cots[pl.ds(s, 64, stride=8), :][:, 0:64].astype(BF16)
            tall = jnp.concatenate([native] * 4, axis=0) * ymask
            crow[32 * s : 32 * s + 32, :] = mmd(up, tall, NT)
        crow_b = crow[...].astype(BF16)
        odd = iota((128, 256), 0) % 2 == 1
        for a in range(2):
            back[:, a] = jnp.where(
                odd,
                mm(crow_b, wback[:, 512 * a + 256 : 512 * a + 512]),
                mm(crow_b, wback[:, 512 * a : 512 * a + 256]),
            ).reshape(16, 8, 256)
        for s in range(4):
            rows = back[4 * s : 4 * s + 4].reshape(64, 256) * masks[64 * s : 64 * s + 64, :]
            slots[s] = rows.astype(BF16).astype(F32)
        place(0, 1, fkg)
        second = halo(0, 1)

        loads[4].wait()
        loads[5].wait()
        gap = jnp.zeros((864, 96), BF16)
        for c in range(2):
            flat = jnp.concatenate([wraw[c].reshape(864, 32), gap], axis=1)
            flat = flat + pltpu.roll(flat, 32, 1)
            wtile[c, 0:864, :] = flat + pltpu.roll(flat, 64, 1)
        lane = iota((32, 128), 1)
        quarter = [one_hot(lane // 32 == k).astype(BF16) for k in range(4)]
        for c in range(2):
            for g in range(7):
                turned = wtile[c, 128 * g : 128 * g + 128, :].T[0:32]
                for k in range(4 if g < 6 else 3):
                    piece = turned * quarter[k]
                    piece = piece + pltpu.roll(piece, 32, 1)
                    at = 32 * (26 - 4 * g - k)
                    wtile[2 + c, at : at + 32, :] = piece + pltpu.roll(piece, 64, 1)

        def band(kind, carry):
            for dx in range(3):
                for dz in range(3):
                    low, mid, high = (
                        wtile[kind, 32 * (9 * dx + 3 * dy + dz) : 32 * (9 * dx + 3 * dy + dz) + 32, :]
                        for dy in range(3)
                    )
                    for j in range(8):
                        at = 512 * (j // 4) + 128 * dz + 32 * (j % 4)
                        for half in range(2):
                            value = None
                            for jo, tap in ((j - 1, high), (j, mid), (j + 1, low)):
                                if 4 * half <= jo < 4 * half + 4:
                                    term = tap * quarter[jo - 4 * half]
                                    value = term if value is None else value + term
                            if value is not None:
                                tmats[kind, dx, at : at + 32, 128 * half : 128 * half + 128] = value
                    at = 384 + 32 * dz
                    tmats[kind, dx, at : at + 32, 0:128] = low * quarter[0]
                    tmats[kind, dx, at + 512 : at + 544, 128:256] = high * quarter[3]
            return carry

        lax.fori_loop(0, 4, band, 0)

        first.wait_recv()
        put_halo(0, 0, fki)
        before = conv(fki, cells, tmats, 0) * masks[...]
        sig = 1.0 / (1.0 + jnp.exp(-before))
        hidden = (before / (1.0 + jnp.exp(-before))).astype(BF16)
        hidden_t = hidden.T
        slope = sig * (1.0 + before * (1.0 - sig)) * masks[...]
        slots[0:4] = hidden.astype(F32).reshape(4, 64, 256)
        place(1, 0, fkh)
        third = halo(1, 0)

        second.wait_recv()
        put_halo(0, 1, fkg)
        grad = (conv(fkg, cells, tmats, 3) * slope).astype(BF16)
        slots[0:4] = grad.astype(F32).reshape(4, 64, 256)
        place(1, 1, fkf)
        fourth = halo(1, 1)

        kernel_grad(grad.T, fki, cells, blocks)
        pack_blocks(blocks, pw, 0)
        kernel_grad(hidden_t, fkg, cells, blocks2)
        pack_blocks(blocks2, pw, 224)
        pw[448:480, :] = jnp.zeros((32, 128), BF16)
        pw[480:512, :] = jnp.zeros((32, 128), BF16)
        for k in range(g1):
            p1[k] = pw[rows_w * k : rows_w * k + rows_w, :]
        q1[m] = p1[m]

        def start_all(src, dst, mine, count, peer, send, recv, by_peer):
            for k in range(1, count):
                other = (mine + k) % count
                pltpu.make_async_remote_copy(
                    src_ref=src.at[other] if by_peer else src,
                    dst_ref=dst.at[mine],
                    send_sem=send,
                    recv_sem=recv,
                    device_id=peer(other),
                    device_id_type=MESH,
                ).start()

        def wait_all(src, dst, mine, count, peer, send, recv, by_peer):
            c = pltpu.make_async_remote_copy(
                src_ref=dst.at[0 : count - 1],
                dst_ref=dst.at[0 : count - 1],
                send_sem=send,
                recv_sem=recv,
                device_id=peer((mine + 1) % count),
                device_id_type=MESH,
            )
            c.wait_recv()
            c.wait_send()

        plan_w1 = (p1, q1, m, g1, peer1, w1s, w1r, True)
        plan_w2 = (p2, q2, u, g2, peer2, w2s, w2r, False)
        plan_w3 = (p3, q3, m, g1, peer1, w3s, w3r, False)
        plan_d1 = (d1, e1, m, g1, peer1, d1s, d1r, True)
        plan_d2 = (d2, e2, u, g2, peer2, d2s, d2r, False)
        plan_d3 = (d3, e3, m, g1, peer1, d3s, d3r, False)

        def added(ref, count):
            total = ref[0].astype(F32)
            for k in range(1, count):
                total = total + ref[k].astype(F32)
            return total

        start_all(*plan_w1)

        third.wait_recv()
        put_halo(1, 0, fkh)
        summed = (inps[...] + conv(fkh, cells, tmats, 1) * masks[...]).reshape(16, 2, 8, 256)
        lhs = jnp.concatenate(
            [summed[:, 0].reshape(128, 256), summed[:, 1].reshape(128, 256)], axis=1
        ).astype(BF16)

        crow_f = crow[...]
        rhs = jnp.concatenate(
            [jnp.where(odd, 0.0, crow_f).astype(BF16), jnp.where(odd, crow_f, 0.0).astype(BF16)], axis=1
        )
        low64 = iota((64, 128), 1) < 64
        for a in range(2):
            mscr[:, 0:512] = mm(lhs[:, 256 * a : 256 * a + 256].T, rhs)
            halves = []
            for d in range(2):
                c0 = 256 * d
                even_part = mscr[0:64, c0 : c0 + 128] + mscr[128:192, c0 + 128 : c0 + 256]
                odd_part = mscr[64:128, c0 : c0 + 128] + mscr[192:256, c0 + 128 : c0 + 256]
                if d == 0:
                    halves.append(even_part + pltpu.roll(odd_part, 64, 1))
                else:
                    halves.append(pltpu.roll(even_part, 64, 1) + odd_part)
            pd[64 * a : 64 * a + 64, :] = jnp.where(low64, halves[0], halves[1])
        for k in range(g1):
            d1[k] = pd[rows_d * k : rows_d * k + rows_d, :]
        e1[m] = d1[m]
        start_all(*plan_d1)

        rows = mm(lhs, wdn[:, 0:256]) + pltpu.roll(mm(lhs, wdn[:, 256:512]), 127, 0)
        rows = rows.astype(BF16)
        for s in range(4):
            wide = mmd(rows[32 * s : 32 * s + 32, :], even, TN)
            total = None
            for y4 in range(4):
                part = jnp.where(iota((64, 64), 1) // 4 % 4 == y4, wide[64 * y4 : 64 * y4 + 64], 0.0)
                total = part if total is None else total + part
            cots[pl.ds(s, 64, stride=8), :] = jnp.concatenate([total, total], axis=1)
        low4 = iota((4, 128), 1) < 64
        for k in range(32):
            o_down[:, 128 * k : 128 * k + 128] = jnp.where(
                low4, cots[pl.ds(16 * k, 4), :], cots[pl.ds(16 * k + 8, 4), :]
            ).astype(BF16)

        wait_all(*plan_w1)
        p2[...] = added(q1, g1).astype(BF16)
        q2[u] = p2[...]
        start_all(*plan_w2)

        fourth.wait_recv()
        put_halo(1, 1, fkf)
        value = (back[...].reshape(256, 256) + conv(fkf, cells, tmats, 2)) * masks[...]
        value = value.astype(BF16)

        wait_all(*plan_d1)
        d2[...] = added(e1, g1)
        e2[u] = d2[...]
        start_all(*plan_d2)

        for c in (first, second, third, fourth):
            c.wait_send()
        jl512 = iota((32, 512), 1) // 8 % 8
        for s in range(4):
            wide = mmd(value[64 * s : 64 * s + 64, :], pick[...], TN)
            total = None
            for j in range(8):
                part = jnp.where(jl512 == j, wide[32 * j : 32 * j + 32], 0.0)
                total = part if total is None else total + part
            o_gf[s] = total.astype(BF16)

        wait_all(*plan_w2)
        p3[...] = (added(q2, g2) * scale).astype(BF16)
        q3[m] = p3[...]
        start_all(*plan_w3)
        wait_all(*plan_d2)
        d3[...] = added(e2, g2) * scale
        e3[m] = d3[...]
        start_all(*plan_d3)

        wait_all(*plan_w3)
        for k in range(g1):
            o_pw[rows_w * k : rows_w * k + rows_w, :] = q3[k]
        wait_all(*plan_d3)
        for k in range(g1):
            o_pd[rows_d * k : rows_d * k + rows_d, :] = e3[k]

    def vm(shape, dtype=F32):
        return pltpu.VMEM(shape, dtype)

    dma = pltpu.SemaphoreType.DMA
    field = vm((8, 96, 1024), BF16)
    scratch = [
        vm((4, 32, 512), BF16), vm((4, 512), jnp.int32), vm((4, 4096), BF16), vm((2, 27, 32, 32), BF16), vm((8, 32, 64), BF16),
        vm((4, 3, 1024, 256), BF16), vm((4, 896, 128), BF16), vm((512, 512), BF16), vm((256, 1024), BF16),
        vm((64, 512), BF16), vm((5, 64, 256)), vm((128, 256)), vm((512, 128)), vm((256, 256)), vm((256, 256)), vm((16, 2, 8, 256)),
        field, field, field, field, vm((256, 1024)), vm((9, 32, 128)), vm((9, 32, 128)),
        vm((2, 2, 416, 128), BF16), vm((2, 2, 416, 128), BF16),
        vm((512, 128), BF16), vm((g1, rows_w, 128), BF16), vm((g1, rows_w, 128), BF16),
        vm((rows_w, 128), BF16), vm((g2, rows_w, 128), BF16), vm((rows_w, 128), BF16), vm((g1, rows_w, 128), BF16),
        vm((128, 128)), vm((g1, rows_d, 128)), vm((g1, rows_d, 128)),
        vm((rows_d, 128)), vm((g2, rows_d, 128)), vm((rows_d, 128)), vm((g1, rows_d, 128)),
        dma((6,)), dma((2, 2)), dma((2, 2)),
        *[dma] * 12,
    ]
    whole = pl.BlockSpec(memory_space=pltpu.VMEM)
    far = pl.BlockSpec(memory_space=pltpu.HBM)
    step = pl.pallas_call(
        body,
        out_shape=(
            jax.ShapeDtypeStruct((512, 128), BF16),
            jax.ShapeDtypeStruct((128, 128), F32),
            jax.ShapeDtypeStruct((4, 32, 512), BF16),
            jax.ShapeDtypeStruct((4, 4096), BF16),
        ),
        in_specs=[pl.BlockSpec(memory_space=pltpu.SMEM)] + [far] * 6,
        out_specs=(whole,) * 4,
        scratch_shapes=scratch,
        compiler_params=pltpu.CompilerParams(
            collective_id=0, has_side_effects=True, vmem_limit_bytes=32 * 1024 * 1024
        ),
    )
    last = pl.pallas_call(
        finish,
        out_shape=(
            jax.ShapeDtypeStruct((4, 4096), BF16),
            jax.ShapeDtypeStruct((4, 32, 512), BF16),
            jax.ShapeDtypeStruct((27, 32, 32), F32),
            jax.ShapeDtypeStruct((27, 32, 32), F32),
            jax.ShapeDtypeStruct((8, 32, 64), F32),
        ),
        in_specs=[whole] * 4,
        out_specs=(whole,) * 5,
        compiler_params=pltpu.CompilerParams(vmem_limit_bytes=8 * 1024 * 1024),
    )

    def on_device(features, voxel_mask, brick_cell, conv_one, conv_two, down_weight, cotangent):
        pw, pd, gf, down = step(
            *[
                pltpu.with_memory_space_constraint(x, pltpu.HBM)
                for x in (brick_cell, features, voxel_mask, cotangent, conv_one, conv_two, down_weight)
            ]
        )
        return last(pw, pd, gf, down)

    return on_device


def solution(mesh):
    rows = P(("region", "tile"), None)
    cube = P(("region", "tile"), None, None)
    in_specs = (cube, rows, P(("region", "tile")), P(), P(), P(), rows)
    out_specs = (rows, cube, P(), P(), P())
    return jax.shard_map(
        build(mesh.shape["region"], mesh.shape["tile"]),
        mesh=mesh,
        in_specs=in_specs,
        out_specs=out_specs,
        check_vma=False,
    )
```

```python
import math

import jax
import jax.numpy as jnp
from jax import lax
from jax.experimental import pallas as pl
from jax.experimental.pallas import tpu as pltpu
from jax.sharding import PartitionSpec as P

MESH = pl.DeviceIdType.MESH
F32 = jnp.float32
BF16 = jnp.bfloat16
NT = (((1,), (1,)), ((), ()))
TN = (((0,), (0,)), ((), ()))


def mm(a, b):
    return jnp.dot(a, b, preferred_element_type=F32)


def mmd(a, b, dims):
    return lax.dot_general(a, b, dims, preferred_element_type=F32)


def iota(shape, dim):
    return lax.broadcasted_iota(jnp.int32, shape, dim)


def one_hot(cond):
    return jnp.where(cond, 1.0, 0.0)


def put(fk, zb, first_x, value, lanes):
    n = value.shape[0] // 8
    for xb in range(2):
        base = 8 * xb
        for a, b in ((base, base + 1), (base + 1, base + 9), (base + 9, base + 10)):
            a, b = max(a, first_x), min(b, first_x + n)
            if a < b:
                part = value[8 * (a - first_x) : 8 * (b - first_x)]
                fk[4 * xb + zb, 8 * (a - base) + 8 : 8 * (b - base) + 8, lanes] = part.astype(BF16)


def put_center(fk, first_x, rows):
    n = rows.shape[0] // 32
    cube = rows.reshape(4 * n, 8, 256)
    down = pltpu.roll(cube, 1, 1).reshape(n, 4, 8, 256)
    up = pltpu.roll(cube, 7, 1).reshape(n, 4, 8, 256)
    cube = cube.reshape(n, 4, 8, 256)
    row = iota((n, 8, 256), 1)
    for zb in range(4):
        below = jnp.where(row > 0, down[:, zb], down[:, zb - 1] if zb > 0 else 0.0)
        above = jnp.where(row < 7, up[:, zb], up[:, zb + 1] if zb < 3 else 0.0)
        for k, part in enumerate((below, cube[:, zb], above)):
            flat = part.reshape(8 * n, 256)
            put(fk, zb, first_x, flat[:, 0:128], slice(128 * k, 128 * k + 128))
            put(fk, zb, first_x, flat[:, 128:256], slice(512 + 128 * k, 640 + 128 * k))


def pack_edge(rows, lane0, lanes):
    n = rows.shape[0] // 32
    cube = rows.reshape(n, 4, 8, 128)
    total = None
    for zb in range(4):
        part = cube[:, zb].reshape(n * 8, 128)
        turn = (32 * zb - lane0) % 128
        if turn:
            part = pltpu.roll(part, turn, 1)
        total = part if total is None else jnp.where(lanes // 32 == zb, part, total)
    return total


def put_edges(fk, first_x, side, packed):
    n = packed.shape[0] // 8
    lane = iota((n * 8, 128), 1)
    row = iota((n * 8, 128), 0) % 8
    cube = packed.reshape(n, 8, 128)
    down = pltpu.roll(cube, 1, 1).reshape(n * 8, 128)
    down = jnp.where(row > 0, down, jnp.where(lane >= 32, pltpu.roll(down, 32, 1), 0.0))
    up = pltpu.roll(cube, 7, 1).reshape(n * 8, 128)
    up = jnp.where(row < 7, up, jnp.where(lane < 96, pltpu.roll(up, 96, 1), 0.0))
    for zb in range(4):
        value = 0.0
        for k, part in ((2, up), (1, packed), (0, down)):
            turn = (32 * k - 32 * zb) % 128
            value = jnp.where(lane < 32 * k + 32, pltpu.roll(part, turn, 1) if turn else part, value)
        at = 512 * side + 384
        put(fk, zb, first_x, value, slice(at, at + 128))


def window(fk, cells, dx):
    return jnp.concatenate([fk[e, 8 * dx + 8 : 8 * dx + 72, :] for e in cells], axis=0)


def conv(fk, cells, t_ref, kind):
    total = None
    for dx in range(3):
        term = mm(window(fk, cells, dx), t_ref[kind, dx])
        total = term if total is None else total + term
    return total


def kernel_grad(xt, fk, cells, blocks):
    lane = iota((32, 128), 1)
    for dx in range(3):
        near = window(fk, cells, dx)
        low = mm(xt[0:160], near[:, 0:512])
        high = mm(xt[96:256], near[:, 512:1024])
        for dz in range(3):
            lo = [low[32 * j : 32 * j + 32, 128 * dz : 128 * dz + 128] for j in range(5)]
            hi = [high[32 * j : 32 * j + 32, 128 * dz : 128 * dz + 128] for j in range(5)]
            still = lo[1] + hi[2]
            back = lo[2] + hi[3]
            half = jnp.where(lane >= 64, lo[3] + hi[4], jnp.where(lane < 32, hi[0], 0.0))
            ahead = jnp.where(lane >= 96, lo[4], jnp.where(lane < 64, hi[1] + lo[0], 0.0))
            mine = lane // 32 == dz
            first = jnp.where(mine, low[0:32, 384:512], 0.0)
            last = jnp.where(mine, high[128:160, 384:512], 0.0)
            if dz == 0:
                still, half = still + first, half + last
            elif dz == 1:
                back, ahead = back + first, ahead + last
            else:
                half, still = half + first, still + last
            blocks[3 * dx + dz] = (
                still + pltpu.roll(back, 96, 1) + pltpu.roll(half, 64, 1) + pltpu.roll(ahead, 32, 1)
            )


def pack_blocks(blocks, dst, first):
    lane = iota((32, 128), 1)
    for g in range(7):
        value = blocks[g]
        if g < 6:
            extra = pltpu.roll(blocks[7 + g // 3], 32 * (3 - g % 3), 1)
            value = jnp.where(lane < 96, value, extra)
        dst[first + 32 * g : first + 32 * g + 32, :] = value.astype(BF16)


def tap_of(group, slot):
    block, dy = (group, slot) if slot < 3 else (7 + group // 3, group % 3)
    return 9 * (block // 3) + 3 * dy + block % 3


def finish(pw, pd, gf, down, o_down, o_gf, o_w1, o_w2, o_wd):
    for g in range(7):
        one = pw[32 * g : 32 * g + 32, :].astype(F32).T
        two = pw[224 + 32 * g : 224 + 32 * g + 32, :].astype(F32)
        for slot in range(4 if g < 6 else 3):
            k = tap_of(g, slot)
            o_w1[k] = one[32 * slot : 32 * slot + 32, :]
            o_w2[26 - k] = two[:, 32 * slot : 32 * slot + 32]
    for a in range(2):
        for b in range(2):
            for d in range(2):
                o_wd[4 * a + 2 * b + d] = pd[64 * a + 32 * b : 64 * a + 32 * b + 32, 64 * d : 64 * d + 64]
    o_gf[...] = gf[...]
    o_down[...] = down[...]


def build(n_r, n_t):
    inner = min(16, n_t)
    outer = n_t // inner
    g1 = n_r * outer
    g2 = inner
    rows_w = 512 // g1
    rows_d = 128 // g1
    scale = 1.0 / math.sqrt(4 * n_r * n_t * 512.0)

    def body(
        bc, feat_h, vmask_h, cot_h, one_h, two_h, dw_h,
        o_pw, o_pd, o_gf, o_down,
        feat, vmask, cot, wraw, dw,
        tmats, wtile, wdn, wback, pick, slots, crow, cots, inps, masks, back,
        fki, fkg, fkh, fkf, mscr, blocks, blocks2,
        sbuf, rbuf,
        pw, p1, q1, p2, q2, p3, q3, pd, d1, e1, d2, e2, d3, e3,
        ins, hs, hr, w1s, w1r, w2s, w2r, w3s, w3r, d1s, d1r, d2s, d2r, d3s, d3r,
    ):
        loads = [
            pltpu.make_async_copy(src, dst, ins.at[k])
            for k, (src, dst) in enumerate(
                [(feat_h, feat), (vmask_h, vmask), (cot_h, cot), (dw_h, dw), (one_h, wraw.at[0]), (two_h, wraw.at[1])]
            )
        ]
        for c in loads:
            c.start()
        r = lax.axis_index("region")
        t = lax.axis_index("tile")
        y = t // inner
        u = t % inner
        m = r * outer + y

        def peer1(k):
            return (k // outer, (k % outer) * inner + u)

        def peer2(k):
            return (r, y * inner + k)

        near = [(dr, dt) for dr in (-1, 0, 1) for dt in (-1, 0, 1) if (dr, dt) != (0, 0)]

        def neighbour(dr, dt):
            return ((r + dr + n_r) % n_r, (t + dt + n_t) % n_t)

        barrier = pltpu.get_barrier_semaphore()
        for dr, dt in near:
            pl.semaphore_signal(barrier, inc=1, device_id=neighbour(dr, dt), device_id_type=MESH)

        def greet1(k, carry):
            pl.semaphore_signal(barrier, inc=1, device_id=peer1((m + k) % g1), device_id_type=MESH)
            return carry

        def greet2(k, carry):
            pl.semaphore_signal(barrier, inc=1, device_id=peer2((u + k) % g2), device_id_type=MESH)
            return carry

        lax.fori_loop(1, g1, greet1, 0)
        lax.fori_loop(1, g2, greet2, 0)

        cells = [jnp.maximum(bc[s], 0) for s in range(4)]
        lives = [jnp.where(bc[s] >= 0, 1.0, 0.0) for s in range(4)]
        owners = []
        for e in range(8):
            owner = jnp.int32(4)
            for s in range(4):
                owner = jnp.where(bc[s] == e, jnp.int32(s), owner)
            owners.append(owner)

        nothing = jnp.zeros((32, 128), BF16)
        for c in range(2):
            wtile[c, 864:896, :] = nothing
        for kind in range(4):
            for dx in range(3):
                for at in range(0, 1024, 32):
                    high_row = at >= 512
                    inner_row = at % 512 < 384
                    j = at % 128 // 32 + 4 * high_row
                    for half in range(2):
                        pad = at % 512 == 480
                        full = 4 * half - 1 <= j <= 4 * half + 4 if inner_row else half == high_row
                        if pad or not full:
                            tmats[kind, dx, at : at + 32, 128 * half : 128 * half + 128] = nothing

        v = iota((64, 512), 1)
        w = iota((64, 512), 0)
        pick[...] = one_hot((v // 64 == w // 8) & (v % 8 == w % 8)).astype(BF16)
        jlane = iota((32, 128), 1) // 8 % 8
        jmask = [jnp.concatenate([one_hot(jlane == j).astype(BF16)] * 4, axis=1) for j in range(8)]
        jcols = one_hot(iota((64, 256), 0) // 8 == iota((64, 256), 1) // 32).astype(BF16)
        jcols = jnp.concatenate([jcols] * 8, axis=0)
        cv = iota((32, 64), 1)
        cw = iota((32, 64), 0)
        up = one_hot((cv // 16 == cw // 8) & (cv % 4 == cw % 8 // 2)).astype(BF16)
        even = one_hot((cv // 16 == cw // 8) & (2 * (cv % 4) == cw % 8)).astype(BF16)
        ymask = one_hot(iota((256, 64), 1) // 4 % 4 == iota((256, 64), 0) // 64).astype(BF16)
        slots[4] = jnp.zeros((64, 256), F32)

        def halo(phase, field):
            plan = [
                (256, 320, 64, (-1, 0)),
                (320, 256, 64, (1, 0)),
                (0, 128, 128, (0, -1)),
                (128, 0, 128, (0, 1)),
                (384, 408, 8, (-1, -1)),
                (392, 400, 8, (-1, 1)),
                (400, 392, 8, (1, -1)),
                (408, 384, 8, (1, 1)),
            ]
            copies = [
                pltpu.make_async_remote_copy(
                    src_ref=sbuf.at[phase, field, src : src + size],
                    dst_ref=rbuf.at[phase, field, dst : dst + size],
                    send_sem=hs.at[phase, field],
                    recv_sem=hr.at[phase, field],
                    device_id=neighbour(dr, dt),
                    device_id_type=MESH,
                )
                for src, dst, size, (dr, dt) in plan
            ]
            for c in copies:
                c.start()
            return pltpu.make_async_remote_copy(
                src_ref=sbuf.at[phase, field],
                dst_ref=rbuf.at[phase, field],
                send_sem=hs.at[phase, field],
                recv_sem=hr.at[phase, field],
                device_id=neighbour(0, 1),
                device_id_type=MESH,
            )

        def place(phase, field, fk):
            lanes = iota((64, 128), 1)
            for part in range(2):
                rows = jnp.concatenate(
                    [slots[owners[4 * part + zb]].reshape(8, 1, 8, 256) for zb in range(4)], axis=1
                ).reshape(256, 256)
                put_center(fk, 1 + 8 * part, rows)
                low = pack_edge(rows[:, 0:128], 0, lanes)
                high = pack_edge(rows[:, 128:256], 96, lanes)
                sbuf[phase, field, 64 * part : 64 * part + 64, :] = low.astype(BF16)
                sbuf[phase, field, 128 + 64 * part : 192 + 64 * part, :] = high.astype(BF16)
                a = 224 * part
                b = 56 * part
                x = 256 + 64 * part
                sbuf[phase, field, x : x + 32, :] = rows[a : a + 32, 0:128].astype(BF16)
                sbuf[phase, field, x + 32 : x + 64, :] = rows[a : a + 32, 128:256].astype(BF16)
                x = 384 + 16 * part
                sbuf[phase, field, x : x + 8, :] = low[b : b + 8].astype(BF16)
                sbuf[phase, field, x + 8 : x + 16, :] = high[b : b + 8].astype(BF16)

        has = [
            jnp.where(r > 0, 1.0, 0.0),
            jnp.where(r < n_r - 1, 1.0, 0.0),
            jnp.where(t > 0, 1.0, 0.0),
            jnp.where(t < n_t - 1, 1.0, 0.0),
        ]

        def put_halo(phase, field, fk):
            for end in range(2):
                x = 256 + 64 * end
                plane = jnp.concatenate(
                    [rbuf[phase, field, x : x + 32, :], rbuf[phase, field, x + 32 : x + 64, :]], axis=1
                )
                put_center(fk, 17 * end, plane.astype(F32) * has[end])
            for side in range(2):
                face = rbuf[phase, field, 128 * side : 128 * side + 128, :]
                put_edges(fk, 1, side, face.astype(F32) * has[2 + side])
                for end in range(2):
                    x = 384 + 16 * end + 8 * side
                    packed = rbuf[phase, field, x : x + 8, :].astype(F32)
                    put_edges(fk, 17 * end, side, packed * (has[end] * has[2 + side]))

        loads[0].wait()
        loads[1].wait()
        for s in range(4):
            seen = jnp.broadcast_to((vmask[s : s + 1, :].astype(F32) * lives[s]), (64, 512)).astype(BF16)
            masks[64 * s : 64 * s + 64, :] = mm(pick[...] * seen, jcols)
            kept = feat[s] * seen[0:32]
            tall = jnp.concatenate([kept * jmask[j] for j in range(8)], axis=0)
            got = mmd(pick[...], tall, NT)
            inps[64 * s : 64 * s + 64, :] = got
            slots[s] = got
        place(0, 0, fki)
        pl.semaphore_wait(barrier, 8 + (g1 - 1) + (g2 - 1))
        first = halo(0, 0)

        loads[2].wait()
        loads[3].wait()
        dwide = dw[...].reshape(256, 64).astype(F32)
        dtile = jnp.concatenate([dwide, dwide], axis=1)
        lane64 = iota((32, 128), 1) // 64
        for a in range(2):
            for b in range(2):
                for d in range(2):
                    k = 4 * a + 2 * b + d
                    block = dtile[32 * k : 32 * k + 32]
                    for y4 in range(4):
                        row = 256 * a + 32 * (2 * y4 + b)
                        for half in range(2):
                            col = 256 * d + 128 * half
                            if y4 // 2 == half:
                                value = jnp.where(lane64 == y4 % 2, block, 0.0).astype(BF16)
                            else:
                                value = jnp.zeros((32, 128), BF16)
                            wdn[row : row + 32, col : col + 128] = value
        lane32 = iota((64, 128), 1)
        for a in range(2):
            turned = dtile[128 * a : 128 * a + 128, :].T[0:64]
            for d in range(2):
                low = turned if d == 0 else pltpu.roll(turned, 96, 1)
                high = pltpu.roll(turned, 96 - 32 * d, 1)
                pair = jnp.where(lane32 < 32, low, jnp.where(lane32 < 64, high, 0.0))
                pair = pair + pltpu.roll(pair, 64, 1)
                for y4 in range(4):
                    for half in range(2):
                        col = 512 * a + 256 * d + 128 * half
                        if y4 // 2 == half:
                            value = jnp.where(lane32 // 64 == y4 % 2, pair, 0.0).astype(BF16)
                        else:
                            value = jnp.zeros((64, 128), BF16)
                        wback[64 * y4 : 64 * y4 + 64, col : col + 128] = value

        for k in range(32):
            part = cot[:, 128 * k : 128 * k + 128].astype(F32)
            cots[pl.ds(16 * k, 4), :] = part
            cots[pl.ds(16 * k + 8, 4), :] = pltpu.roll(part, 64, 1)
        for s in range(4):
            native = cots[pl.ds(s, 64, stride=8), :][:, 0:64].astype(BF16)
            tall = jnp.concatenate([native] * 4, axis=0) * ymask
            crow[32 * s : 32 * s + 32, :] = mmd(up, tall, NT)
        crow_b = crow[...].astype(BF16)
        odd = iota((128, 256), 0) % 2 == 1
        for a in range(2):
            back[:, a] = jnp.where(
                odd,
                mm(crow_b, wback[:, 512 * a + 256 : 512 * a + 512]),
                mm(crow_b, wback[:, 512 * a : 512 * a + 256]),
            ).reshape(16, 8, 256)
        for s in range(4):
            rows = back[4 * s : 4 * s + 4].reshape(64, 256) * masks[64 * s : 64 * s + 64, :]
            slots[s] = rows.astype(BF16).astype(F32)
        place(0, 1, fkg)
        second = halo(0, 1)

        loads[4].wait()
        loads[5].wait()
        gap = jnp.zeros((864, 96), BF16)
        for c in range(2):
            flat = jnp.concatenate([wraw[c].reshape(864, 32), gap], axis=1)
            flat = flat + pltpu.roll(flat, 32, 1)
            wtile[c, 0:864, :] = flat + pltpu.roll(flat, 64, 1)
        lane = iota((32, 128), 1)
        quarter = [one_hot(lane // 32 == k).astype(BF16) for k in range(4)]
        wide = [jnp.concatenate([q] * 4, axis=0) for q in quarter]
        for c in range(2):
            for pack in range(2):
                groups = range(4 * pack, min(4 * pack + 4, 7))
                value = None
                for g in groups:
                    term = wtile[c, 128 * g : 128 * g + 128, :] * wide[g % 4]
                    value = term if value is None else value + term
                turned = value.T
                for g in groups:
                    mine = turned[32 * (g % 4) : 32 * (g % 4) + 32]
                    for k in range(4 if g < 6 else 3):
                        piece = mine * quarter[k]
                        piece = piece + pltpu.roll(piece, 32, 1)
                        at = 32 * (26 - 4 * g - k)
                        wtile[2 + c, at : at + 32, :] = piece + pltpu.roll(piece, 64, 1)

        def band(kind, carry):
            for dx in range(3):
                for dz in range(3):
                    low, mid, high = (
                        wtile[kind, 32 * (9 * dx + 3 * dy + dz) : 32 * (9 * dx + 3 * dy + dz) + 32, :]
                        for dy in range(3)
                    )
                    for j in range(8):
                        at = 512 * (j // 4) + 128 * dz + 32 * (j % 4)
                        for half in range(2):
                            value = None
                            for jo, tap in ((j - 1, high), (j, mid), (j + 1, low)):
                                if 4 * half <= jo < 4 * half + 4:
                                    term = tap * quarter[jo - 4 * half]
                                    value = term if value is None else value + term
                            if value is not None:
                                tmats[kind, dx, at : at + 32, 128 * half : 128 * half + 128] = value
                    at = 384 + 32 * dz
                    tmats[kind, dx, at : at + 32, 0:128] = low * quarter[0]
                    tmats[kind, dx, at + 512 : at + 544, 128:256] = high * quarter[3]
            return carry

        lax.fori_loop(0, 4, band, 0)

        first.wait_recv()
        put_halo(0, 0, fki)
        before = conv(fki, cells, tmats, 0) * masks[...]
        sig = 1.0 / (1.0 + jnp.exp(-before))
        hidden = (before / (1.0 + jnp.exp(-before))).astype(BF16)
        hidden_t = hidden.T
        slope = sig * (1.0 + before * (1.0 - sig)) * masks[...]
        slots[0:4] = hidden.astype(F32).reshape(4, 64, 256)
        place(1, 0, fkh)
        third = halo(1, 0)

        second.wait_recv()
        put_halo(0, 1, fkg)
        grad = (conv(fkg, cells, tmats, 3) * slope).astype(BF16)
        slots[0:4] = grad.astype(F32).reshape(4, 64, 256)
        place(1, 1, fkf)
        fourth = halo(1, 1)

        kernel_grad(grad.T, fki, cells, blocks)
        pack_blocks(blocks, pw, 0)
        kernel_grad(hidden_t, fkg, cells, blocks2)
        pack_blocks(blocks2, pw, 224)
        pw[448:480, :] = jnp.zeros((32, 128), BF16)
        pw[480:512, :] = jnp.zeros((32, 128), BF16)
        for k in range(g1):
            p1[k] = pw[rows_w * k : rows_w * k + rows_w, :]
        q1[m] = p1[m]

        def start_all(src, dst, mine, count, peer, send, recv, by_peer):
            slow, fast = (n_r, outer) if peer is peer1 else (g2 // 2, 2)
            steps = [(a, b) for a in range(slow) for b in range(fast) if (a, b) != (0, 0)]
            hops = (lambda b: min(b, fast - b)) if peer is peer1 else (lambda b: 0)
            steps.sort(key=lambda ab: -min(ab[0], slow - ab[0]) - hops(ab[1]))
            for a, b in steps:
                other = (mine // fast + a) % slow * fast + (mine % fast + b) % fast
                pltpu.make_async_remote_copy(
                    src_ref=src.at[other] if by_peer else src,
                    dst_ref=dst.at[mine],
                    send_sem=send,
                    recv_sem=recv,
                    device_id=peer(other),
                    device_id_type=MESH,
                ).start()

        def wait_all(src, dst, mine, count, peer, send, recv, by_peer):
            c = pltpu.make_async_remote_copy(
                src_ref=dst.at[0 : count - 1],
                dst_ref=dst.at[0 : count - 1],
                send_sem=send,
                recv_sem=recv,
                device_id=peer((mine + 1) % count),
                device_id_type=MESH,
            )
            c.wait_recv()
            c.wait_send()

        plan_w1 = (p1, q1, m, g1, peer1, w1s, w1r, True)
        plan_w2 = (p2, q2, u, g2, peer2, w2s, w2r, False)
        plan_w3 = (p3, q3, m, g1, peer1, w3s, w3r, False)
        plan_d1 = (d1, e1, m, g1, peer1, d1s, d1r, True)
        plan_d2 = (d2, e2, u, g2, peer2, d2s, d2r, False)
        plan_d3 = (d3, e3, m, g1, peer1, d3s, d3r, False)

        def added(ref, count):
            total = ref[0].astype(F32)
            for k in range(1, count):
                total = total + ref[k].astype(F32)
            return total

        start_all(*plan_w1)

        third.wait_recv()
        put_halo(1, 0, fkh)
        summed = (inps[...] + conv(fkh, cells, tmats, 1) * masks[...]).reshape(16, 2, 8, 256)
        lhs = jnp.concatenate(
            [summed[:, 0].reshape(128, 256), summed[:, 1].reshape(128, 256)], axis=1
        ).astype(BF16)

        crow_f = crow[...]
        rhs = jnp.concatenate(
            [jnp.where(odd, 0.0, crow_f).astype(BF16), jnp.where(odd, crow_f, 0.0).astype(BF16)], axis=1
        )
        low64 = iota((64, 128), 1) < 64
        for a in range(2):
            mscr[:, 0:512] = mm(lhs[:, 256 * a : 256 * a + 256].T, rhs)
            halves = []
            for d in range(2):
                c0 = 256 * d
                even_part = mscr[0:64, c0 : c0 + 128] + mscr[128:192, c0 + 128 : c0 + 256]
                odd_part = mscr[64:128, c0 : c0 + 128] + mscr[192:256, c0 + 128 : c0 + 256]
                if d == 0:
                    halves.append(even_part + pltpu.roll(odd_part, 64, 1))
                else:
                    halves.append(pltpu.roll(even_part, 64, 1) + odd_part)
            pd[64 * a : 64 * a + 64, :] = jnp.where(low64, halves[0], halves[1])
        for k in range(g1):
            d1[k] = pd[rows_d * k : rows_d * k + rows_d, :].astype(BF16)
        e1[m] = d1[m]
        start_all(*plan_d1)

        rows = mm(lhs, wdn[:, 0:256]) + pltpu.roll(mm(lhs, wdn[:, 256:512]), 127, 0)
        rows = rows.astype(BF16)
        for s in range(4):
            wide = mmd(rows[32 * s : 32 * s + 32, :], even, TN)
            total = None
            for y4 in range(4):
                part = jnp.where(iota((64, 64), 1) // 4 % 4 == y4, wide[64 * y4 : 64 * y4 + 64], 0.0)
                total = part if total is None else total + part
            cots[pl.ds(s, 64, stride=8), :] = jnp.concatenate([total, total], axis=1)
        low4 = iota((4, 128), 1) < 64
        for k in range(32):
            o_down[:, 128 * k : 128 * k + 128] = jnp.where(
                low4, cots[pl.ds(16 * k, 4), :], cots[pl.ds(16 * k + 8, 4), :]
            ).astype(BF16)

        wait_all(*plan_w1)
        p2[...] = added(q1, g1).astype(BF16)
        q2[u] = p2[...]
        start_all(*plan_w2)

        fourth.wait_recv()
        put_halo(1, 1, fkf)
        value = (back[...].reshape(256, 256) + conv(fkf, cells, tmats, 2)) * masks[...]
        value = value.astype(BF16)

        wait_all(*plan_d1)
        d2[...] = added(e1, g1).astype(BF16)
        e2[u] = d2[...]
        start_all(*plan_d2)

        for c in (first, second, third, fourth):
            c.wait_send()
        jl512 = iota((32, 512), 1) // 8 % 8
        for s in range(4):
            wide = mmd(value[64 * s : 64 * s + 64, :], pick[...], TN)
            total = None
            for j in range(8):
                part = jnp.where(jl512 == j, wide[32 * j : 32 * j + 32], 0.0)
                total = part if total is None else total + part
            o_gf[s] = total.astype(BF16)

        wait_all(*plan_w2)
        p3[...] = (added(q2, g2) * scale).astype(BF16)
        q3[m] = p3[...]
        start_all(*plan_w3)
        wait_all(*plan_d2)
        d3[...] = (added(e2, g2) * scale).astype(BF16)
        e3[m] = d3[...]
        start_all(*plan_d3)

        wait_all(*plan_w3)
        for k in range(g1):
            o_pw[rows_w * k : rows_w * k + rows_w, :] = q3[k]
        wait_all(*plan_d3)
        for k in range(g1):
            o_pd[rows_d * k : rows_d * k + rows_d, :] = e3[k].astype(F32)

    def vm(shape, dtype=F32):
        return pltpu.VMEM(shape, dtype)

    dma = pltpu.SemaphoreType.DMA
    field = vm((8, 96, 1024), BF16)
    scratch = [
        vm((4, 32, 512), BF16), vm((4, 512), jnp.int32), vm((4, 4096), BF16), vm((2, 27, 32, 32), BF16), vm((8, 32, 64), BF16),
        vm((4, 3, 1024, 256), BF16), vm((4, 896, 128), BF16), vm((512, 512), BF16), vm((256, 1024), BF16),
        vm((64, 512), BF16), vm((5, 64, 256)), vm((128, 256)), vm((512, 128)), vm((256, 256)), vm((256, 256)), vm((16, 2, 8, 256)),
        field, field, field, field, vm((256, 1024)), vm((9, 32, 128)), vm((9, 32, 128)),
        vm((2, 2, 416, 128), BF16), vm((2, 2, 416, 128), BF16),
        vm((512, 128), BF16), vm((g1, rows_w, 128), BF16), vm((g1, rows_w, 128), BF16),
        vm((rows_w, 128), BF16), vm((g2, rows_w, 128), BF16), vm((rows_w, 128), BF16), vm((g1, rows_w, 128), BF16),
        vm((128, 128)), vm((g1, rows_d, 128), BF16), vm((g1, rows_d, 128), BF16),
        vm((rows_d, 128), BF16), vm((g2, rows_d, 128), BF16), vm((rows_d, 128), BF16), vm((g1, rows_d, 128), BF16),
        dma((6,)), dma((2, 2)), dma((2, 2)),
        *[dma] * 12,
    ]
    whole = pl.BlockSpec(memory_space=pltpu.VMEM)
    far = pl.BlockSpec(memory_space=pltpu.HBM)
    step = pl.pallas_call(
        body,
        out_shape=(
            jax.ShapeDtypeStruct((512, 128), BF16),
            jax.ShapeDtypeStruct((128, 128), F32),
            jax.ShapeDtypeStruct((4, 32, 512), BF16),
            jax.ShapeDtypeStruct((4, 4096), BF16),
        ),
        in_specs=[pl.BlockSpec(memory_space=pltpu.SMEM)] + [far] * 6,
        out_specs=(whole,) * 4,
        scratch_shapes=scratch,
        compiler_params=pltpu.CompilerParams(
            collective_id=0, has_side_effects=True, vmem_limit_bytes=32 * 1024 * 1024
        ),
    )
    last = pl.pallas_call(
        finish,
        out_shape=(
            jax.ShapeDtypeStruct((4, 4096), BF16),
            jax.ShapeDtypeStruct((4, 32, 512), BF16),
            jax.ShapeDtypeStruct((27, 32, 32), F32),
            jax.ShapeDtypeStruct((27, 32, 32), F32),
            jax.ShapeDtypeStruct((8, 32, 64), F32),
        ),
        in_specs=[whole] * 4,
        out_specs=(whole,) * 5,
        compiler_params=pltpu.CompilerParams(vmem_limit_bytes=8 * 1024 * 1024),
    )

    def on_device(features, voxel_mask, brick_cell, conv_one, conv_two, down_weight, cotangent):
        pw, pd, gf, down = step(
            *[
                pltpu.with_memory_space_constraint(x, pltpu.HBM)
                for x in (brick_cell, features, voxel_mask, cotangent, conv_one, conv_two, down_weight)
            ]
        )
        return last(pw, pd, gf, down)

    return on_device


def solution(mesh):
    rows = P(("region", "tile"), None)
    cube = P(("region", "tile"), None, None)
    in_specs = (cube, rows, P(("region", "tile")), P(), P(), P(), rows)
    out_specs = (rows, cube, P(), P(), P())
    return jax.shard_map(
        build(mesh.shape["region"], mesh.shape["tile"]),
        mesh=mesh,
        in_specs=in_specs,
        out_specs=out_specs,
        check_vma=False,
    )
```

```python
import math

import jax
import jax.numpy as jnp
from jax import lax
from jax.experimental import pallas as pl
from jax.experimental.pallas import tpu as pltpu
from jax.sharding import PartitionSpec as P

MESH = pl.DeviceIdType.MESH
F32 = jnp.float32
BF16 = jnp.bfloat16
NT = (((1,), (1,)), ((), ()))
TN = (((0,), (0,)), ((), ()))


def mm(a, b):
    return jnp.dot(a, b, preferred_element_type=F32)


def mmd(a, b, dims):
    return lax.dot_general(a, b, dims, preferred_element_type=F32)


def iota(shape, dim):
    return lax.broadcasted_iota(jnp.int32, shape, dim)


def one_hot(cond):
    return jnp.where(cond, 1.0, 0.0)


def put(fk, zb, first_x, value, lanes):
    n = value.shape[0] // 8
    for xb in range(2):
        base = 8 * xb
        for a, b in ((base, base + 1), (base + 1, base + 9), (base + 9, base + 10)):
            a, b = max(a, first_x), min(b, first_x + n)
            if a < b:
                part = value[8 * (a - first_x) : 8 * (b - first_x)]
                fk[4 * xb + zb, 8 * (a - base) + 8 : 8 * (b - base) + 8, lanes] = part.astype(BF16)


def put_center(fk, first_x, rows):
    n = rows.shape[0] // 32
    cube = rows.reshape(4 * n, 8, 256)
    down = pltpu.roll(cube, 1, 1).reshape(n, 4, 8, 256)
    up = pltpu.roll(cube, 7, 1).reshape(n, 4, 8, 256)
    cube = cube.reshape(n, 4, 8, 256)
    row = iota((n, 8, 256), 1)
    for zb in range(4):
        below = jnp.where(row > 0, down[:, zb], down[:, zb - 1] if zb > 0 else 0.0)
        above = jnp.where(row < 7, up[:, zb], up[:, zb + 1] if zb < 3 else 0.0)
        for k, part in enumerate((below, cube[:, zb], above)):
            flat = part.reshape(8 * n, 256)
            put(fk, zb, first_x, flat[:, 0:128], slice(128 * k, 128 * k + 128))
            put(fk, zb, first_x, flat[:, 128:256], slice(512 + 128 * k, 640 + 128 * k))


def pack_edge(rows, lane0, lanes):
    n = rows.shape[0] // 32
    cube = rows.reshape(n, 4, 8, 128)
    total = None
    for zb in range(4):
        part = cube[:, zb].reshape(n * 8, 128)
        turn = (32 * zb - lane0) % 128
        if turn:
            part = pltpu.roll(part, turn, 1)
        total = part if total is None else jnp.where(lanes // 32 == zb, part, total)
    return total


def put_edges(fk, first_x, side, packed):
    n = packed.shape[0] // 8
    lane = iota((n * 8, 128), 1)
    row = iota((n * 8, 128), 0) % 8
    cube = packed.reshape(n, 8, 128)
    down = pltpu.roll(cube, 1, 1).reshape(n * 8, 128)
    down = jnp.where(row > 0, down, jnp.where(lane >= 32, pltpu.roll(down, 32, 1), 0.0))
    up = pltpu.roll(cube, 7, 1).reshape(n * 8, 128)
    up = jnp.where(row < 7, up, jnp.where(lane < 96, pltpu.roll(up, 96, 1), 0.0))
    for zb in range(4):
        value = 0.0
        for k, part in ((2, up), (1, packed), (0, down)):
            turn = (32 * k - 32 * zb) % 128
            value = jnp.where(lane < 32 * k + 32, pltpu.roll(part, turn, 1) if turn else part, value)
        at = 512 * side + 384
        put(fk, zb, first_x, value, slice(at, at + 128))


def window(fk, cells, dx):
    return jnp.concatenate([fk[e, 8 * dx + 8 : 8 * dx + 72, :] for e in cells], axis=0)


def conv(fk, cells, t_ref, kind):
    total = None
    for dx in range(3):
        term = mm(window(fk, cells, dx), t_ref[kind, dx])
        total = term if total is None else total + term
    return total


def kernel_grad(xt, fk, cells, blocks):
    lane = iota((32, 128), 1)
    for dx in range(3):
        near = window(fk, cells, dx)
        low = mm(xt[0:160], near[:, 0:512])
        high = mm(xt[96:256], near[:, 512:1024])
        for dz in range(3):
            lo = [low[32 * j : 32 * j + 32, 128 * dz : 128 * dz + 128] for j in range(5)]
            hi = [high[32 * j : 32 * j + 32, 128 * dz : 128 * dz + 128] for j in range(5)]
            still = lo[1] + hi[2]
            back = lo[2] + hi[3]
            half = jnp.where(lane >= 64, lo[3] + hi[4], jnp.where(lane < 32, hi[0], 0.0))
            ahead = jnp.where(lane >= 96, lo[4], jnp.where(lane < 64, hi[1] + lo[0], 0.0))
            mine = lane // 32 == dz
            first = jnp.where(mine, low[0:32, 384:512], 0.0)
            last = jnp.where(mine, high[128:160, 384:512], 0.0)
            if dz == 0:
                still, half = still + first, half + last
            elif dz == 1:
                back, ahead = back + first, ahead + last
            else:
                half, still = half + first, still + last
            blocks[3 * dx + dz] = (
                still + pltpu.roll(back, 96, 1) + pltpu.roll(half, 64, 1) + pltpu.roll(ahead, 32, 1)
            )


def pack_blocks(blocks, dst, first):
    lane = iota((32, 128), 1)
    for g in range(7):
        value = blocks[g]
        if g < 6:
            extra = pltpu.roll(blocks[7 + g // 3], 32 * (3 - g % 3), 1)
            value = jnp.where(lane < 96, value, extra)
        dst[first + 32 * g : first + 32 * g + 32, :] = value.astype(BF16)


def tap_of(group, slot):
    block, dy = (group, slot) if slot < 3 else (7 + group // 3, group % 3)
    return 9 * (block // 3) + 3 * dy + block % 3


def finish(pw, pd, gf, down, o_down, o_gf, o_w1, o_w2, o_wd):
    for g in range(7):
        one = pw[32 * g : 32 * g + 32, :].astype(F32).T
        two = pw[224 + 32 * g : 224 + 32 * g + 32, :].astype(F32)
        for slot in range(4 if g < 6 else 3):
            k = tap_of(g, slot)
            o_w1[k] = one[32 * slot : 32 * slot + 32, :]
            o_w2[26 - k] = two[:, 32 * slot : 32 * slot + 32]
    for a in range(2):
        for b in range(2):
            for d in range(2):
                o_wd[4 * a + 2 * b + d] = pd[64 * a + 32 * b : 64 * a + 32 * b + 32, 64 * d : 64 * d + 64]
    o_gf[...] = gf[...]
    o_down[...] = down[...]


def build(n_r, n_t):
    inner = min(16, n_t)
    outer = n_t // inner
    g1 = n_r * outer
    g2 = inner
    rows_w = 512 // g1
    rows_d = 128 // g1
    scale = 1.0 / math.sqrt(4 * n_r * n_t * 512.0)

    def body(
        bc_h, feat_h, vmask_h, cot_h, one_h, two_h, dw_h,
        o_pw, o_pd, o_gf, o_down,
        bc, feat, vmask, cot, wraw, dw,
        tmats, wtile, wdn, wback, pick, slots, crow, cots, inps, masks, back,
        fki, fkg, fkh, fkf, mscr, blocks, blocks2,
        sbuf, rbuf,
        pw, p1, q1, p2, q2, p3, q3, pd, d1, e1, d2, e2, d3, e3,
        ins, hs, hr, w1s, w1r, w2s, w2r, w3s, w3r, d1s, d1r, d2s, d2r, d3s, d3r,
    ):
        loads = [
            pltpu.make_async_copy(src, dst, ins.at[k])
            for k, (src, dst) in enumerate(
                [(feat_h, feat), (vmask_h, vmask), (cot_h, cot), (dw_h, dw), (one_h, wraw.at[0]), (two_h, wraw.at[1]), (bc_h, bc)]
            )
        ]
        for c in loads:
            c.start()
        r = lax.axis_index("region")
        t = lax.axis_index("tile")
        y = t // inner
        u = t % inner
        m = r * outer + y

        def peer1(k):
            return (k // outer, (k % outer) * inner + u)

        def peer2(k):
            return (r, y * inner + k)

        near = [(dr, dt) for dr in (-1, 0, 1) for dt in (-1, 0, 1) if (dr, dt) != (0, 0)]

        def neighbour(dr, dt):
            return ((r + dr + n_r) % n_r, (t + dt + n_t) % n_t)

        barrier = pltpu.get_barrier_semaphore()
        for dr, dt in near:
            pl.semaphore_signal(barrier, inc=1, device_id=neighbour(dr, dt), device_id_type=MESH)

        def greet1(k, carry):
            pl.semaphore_signal(barrier, inc=1, device_id=peer1((m + k) % g1), device_id_type=MESH)
            return carry

        def greet2(k, carry):
            pl.semaphore_signal(barrier, inc=1, device_id=peer2((u + k) % g2), device_id_type=MESH)
            return carry

        lax.fori_loop(1, g1, greet1, 0)
        lax.fori_loop(1, g2, greet2, 0)

        nothing = jnp.zeros((32, 128), BF16)
        for c in range(2):
            wtile[c, 864:896, :] = nothing
        for kind in range(4):
            for dx in range(3):
                for at in range(0, 1024, 32):
                    high_row = at >= 512
                    inner_row = at % 512 < 384
                    j = at % 128 // 32 + 4 * high_row
                    for half in range(2):
                        pad = at % 512 == 480
                        full = 4 * half - 1 <= j <= 4 * half + 4 if inner_row else half == high_row
                        if pad or not full:
                            tmats[kind, dx, at : at + 32, 128 * half : 128 * half + 128] = nothing

        v = iota((64, 512), 1)
        w = iota((64, 512), 0)
        pick[...] = one_hot((v // 64 == w // 8) & (v % 8 == w % 8)).astype(BF16)
        jlane = iota((32, 128), 1) // 8 % 8
        jmask = [jnp.concatenate([one_hot(jlane == j).astype(BF16)] * 4, axis=1) for j in range(8)]
        jcols = one_hot(iota((64, 256), 0) // 8 == iota((64, 256), 1) // 32).astype(BF16)
        jcols = jnp.concatenate([jcols] * 8, axis=0)
        cv = iota((32, 64), 1)
        cw = iota((32, 64), 0)
        up = one_hot((cv // 16 == cw // 8) & (cv % 4 == cw % 8 // 2)).astype(BF16)
        even = one_hot((cv // 16 == cw // 8) & (2 * (cv % 4) == cw % 8)).astype(BF16)
        ymask = one_hot(iota((256, 64), 1) // 4 % 4 == iota((256, 64), 0) // 64).astype(BF16)
        slots[4] = jnp.zeros((64, 256), F32)

        def halo(phase, field):
            plan = [
                (256, 320, 64, (-1, 0)),
                (320, 256, 64, (1, 0)),
                (0, 128, 128, (0, -1)),
                (128, 0, 128, (0, 1)),
                (384, 408, 8, (-1, -1)),
                (392, 400, 8, (-1, 1)),
                (400, 392, 8, (1, -1)),
                (408, 384, 8, (1, 1)),
            ]
            copies = [
                pltpu.make_async_remote_copy(
                    src_ref=sbuf.at[phase, field, src : src + size],
                    dst_ref=rbuf.at[phase, field, dst : dst + size],
                    send_sem=hs.at[phase, field],
                    recv_sem=hr.at[phase, field],
                    device_id=neighbour(dr, dt),
                    device_id_type=MESH,
                )
                for src, dst, size, (dr, dt) in plan
            ]
            for c in copies:
                c.start()
            return pltpu.make_async_remote_copy(
                src_ref=sbuf.at[phase, field],
                dst_ref=rbuf.at[phase, field],
                send_sem=hs.at[phase, field],
                recv_sem=hr.at[phase, field],
                device_id=neighbour(0, 1),
                device_id_type=MESH,
            )

        def place(phase, field, fk):
            lanes = iota((64, 128), 1)
            for part in range(2):
                rows = jnp.concatenate(
                    [slots[owners[4 * part + zb]].reshape(8, 1, 8, 256) for zb in range(4)], axis=1
                ).reshape(256, 256)
                put_center(fk, 1 + 8 * part, rows)
                low = pack_edge(rows[:, 0:128], 0, lanes)
                high = pack_edge(rows[:, 128:256], 96, lanes)
                sbuf[phase, field, 64 * part : 64 * part + 64, :] = low.astype(BF16)
                sbuf[phase, field, 128 + 64 * part : 192 + 64 * part, :] = high.astype(BF16)
                a = 224 * part
                b = 56 * part
                x = 256 + 64 * part
                sbuf[phase, field, x : x + 32, :] = rows[a : a + 32, 0:128].astype(BF16)
                sbuf[phase, field, x + 32 : x + 64, :] = rows[a : a + 32, 128:256].astype(BF16)
                x = 384 + 16 * part
                sbuf[phase, field, x : x + 8, :] = low[b : b + 8].astype(BF16)
                sbuf[phase, field, x + 8 : x + 16, :] = high[b : b + 8].astype(BF16)

        has = [
            jnp.where(r > 0, 1.0, 0.0),
            jnp.where(r < n_r - 1, 1.0, 0.0),
            jnp.where(t > 0, 1.0, 0.0),
            jnp.where(t < n_t - 1, 1.0, 0.0),
        ]

        def put_halo(phase, field, fk):
            for end in range(2):
                x = 256 + 64 * end
                plane = jnp.concatenate(
                    [rbuf[phase, field, x : x + 32, :], rbuf[phase, field, x + 32 : x + 64, :]], axis=1
                )
                put_center(fk, 17 * end, plane.astype(F32) * has[end])
            for side in range(2):
                face = rbuf[phase, field, 128 * side : 128 * side + 128, :]
                put_edges(fk, 1, side, face.astype(F32) * has[2 + side])
                for end in range(2):
                    x = 384 + 16 * end + 8 * side
                    packed = rbuf[phase, field, x : x + 8, :].astype(F32)
                    put_edges(fk, 17 * end, side, packed * (has[end] * has[2 + side]))

        loads[6].wait()
        cells = [jnp.maximum(bc[s], 0) for s in range(4)]
        lives = [jnp.where(bc[s] >= 0, 1.0, 0.0) for s in range(4)]
        owners = []
        for e in range(8):
            owner = jnp.int32(4)
            for s in range(4):
                owner = jnp.where(bc[s] == e, jnp.int32(s), owner)
            owners.append(owner)

        loads[0].wait()
        loads[1].wait()
        for s in range(4):
            seen = jnp.broadcast_to((vmask[s : s + 1, :].astype(F32) * lives[s]), (64, 512)).astype(BF16)
            masks[64 * s : 64 * s + 64, :] = mm(pick[...] * seen, jcols)
            kept = feat[s] * seen[0:32]
            tall = jnp.concatenate([kept * jmask[j] for j in range(8)], axis=0)
            got = mmd(pick[...], tall, NT)
            inps[64 * s : 64 * s + 64, :] = got
            slots[s] = got
        place(0, 0, fki)
        pl.semaphore_wait(barrier, 8 + (g1 - 1) + (g2 - 1))
        first = halo(0, 0)

        loads[2].wait()
        loads[3].wait()
        dwide = dw[...].reshape(256, 64).astype(F32)
        dtile = jnp.concatenate([dwide, dwide], axis=1)
        lane64 = iota((32, 128), 1) // 64
        for a in range(2):
            for b in range(2):
                for d in range(2):
                    k = 4 * a + 2 * b + d
                    block = dtile[32 * k : 32 * k + 32]
                    for y4 in range(4):
                        row = 256 * a + 32 * (2 * y4 + b)
                        for half in range(2):
                            col = 256 * d + 128 * half
                            if y4 // 2 == half:
                                value = jnp.where(lane64 == y4 % 2, block, 0.0).astype(BF16)
                            else:
                                value = jnp.zeros((32, 128), BF16)
                            wdn[row : row + 32, col : col + 128] = value
        lane32 = iota((64, 128), 1)
        for a in range(2):
            turned = dtile[128 * a : 128 * a + 128, :].T[0:64]
            for d in range(2):
                low = turned if d == 0 else pltpu.roll(turned, 96, 1)
                high = pltpu.roll(turned, 96 - 32 * d, 1)
                pair = jnp.where(lane32 < 32, low, jnp.where(lane32 < 64, high, 0.0))
                pair = pair + pltpu.roll(pair, 64, 1)
                for y4 in range(4):
                    for half in range(2):
                        col = 512 * a + 256 * d + 128 * half
                        if y4 // 2 == half:
                            value = jnp.where(lane32 // 64 == y4 % 2, pair, 0.0).astype(BF16)
                        else:
                            value = jnp.zeros((64, 128), BF16)
                        wback[64 * y4 : 64 * y4 + 64, col : col + 128] = value

        for k in range(32):
            part = cot[:, 128 * k : 128 * k + 128].astype(F32)
            cots[pl.ds(16 * k, 4), :] = part
            cots[pl.ds(16 * k + 8, 4), :] = pltpu.roll(part, 64, 1)
        for s in range(4):
            native = cots[pl.ds(s, 64, stride=8), :][:, 0:64].astype(BF16)
            tall = jnp.concatenate([native] * 4, axis=0) * ymask
            crow[32 * s : 32 * s + 32, :] = mmd(up, tall, NT)
        crow_b = crow[...].astype(BF16)
        odd = iota((128, 256), 0) % 2 == 1
        for a in range(2):
            back[:, a] = jnp.where(
                odd,
                mm(crow_b, wback[:, 512 * a + 256 : 512 * a + 512]),
                mm(crow_b, wback[:, 512 * a : 512 * a + 256]),
            ).reshape(16, 8, 256)
        for s in range(4):
            rows = back[4 * s : 4 * s + 4].reshape(64, 256) * masks[64 * s : 64 * s + 64, :]
            slots[s] = rows.astype(BF16).astype(F32)
        place(0, 1, fkg)
        second = halo(0, 1)

        loads[4].wait()
        loads[5].wait()
        gap = jnp.zeros((864, 96), BF16)
        for c in range(2):
            flat = jnp.concatenate([wraw[c].reshape(864, 32), gap], axis=1)
            flat = flat + pltpu.roll(flat, 32, 1)
            wtile[c, 0:864, :] = flat + pltpu.roll(flat, 64, 1)
        lane = iota((32, 128), 1)
        quarter = [one_hot(lane // 32 == k).astype(BF16) for k in range(4)]
        wide = [jnp.concatenate([q] * 4, axis=0) for q in quarter]
        for c in range(2):
            for pack in range(2):
                groups = range(4 * pack, min(4 * pack + 4, 7))
                value = None
                for g in groups:
                    term = wtile[c, 128 * g : 128 * g + 128, :] * wide[g % 4]
                    value = term if value is None else value + term
                turned = value.T
                for g in groups:
                    mine = turned[32 * (g % 4) : 32 * (g % 4) + 32]
                    for k in range(4 if g < 6 else 3):
                        piece = mine * quarter[k]
                        piece = piece + pltpu.roll(piece, 32, 1)
                        at = 32 * (26 - 4 * g - k)
                        wtile[2 + c, at : at + 32, :] = piece + pltpu.roll(piece, 64, 1)

        def band(kind, carry):
            for dx in range(3):
                for dz in range(3):
                    low, mid, high = (
                        wtile[kind, 32 * (9 * dx + 3 * dy + dz) : 32 * (9 * dx + 3 * dy + dz) + 32, :]
                        for dy in range(3)
                    )
                    for j in range(8):
                        at = 512 * (j // 4) + 128 * dz + 32 * (j % 4)
                        for half in range(2):
                            value = None
                            for jo, tap in ((j - 1, high), (j, mid), (j + 1, low)):
                                if 4 * half <= jo < 4 * half + 4:
                                    term = tap * quarter[jo - 4 * half]
                                    value = term if value is None else value + term
                            if value is not None:
                                tmats[kind, dx, at : at + 32, 128 * half : 128 * half + 128] = value
                    at = 384 + 32 * dz
                    tmats[kind, dx, at : at + 32, 0:128] = low * quarter[0]
                    tmats[kind, dx, at + 512 : at + 544, 128:256] = high * quarter[3]
            return carry

        lax.fori_loop(0, 4, band, 0)

        first.wait_recv()
        put_halo(0, 0, fki)
        before = conv(fki, cells, tmats, 0) * masks[...]
        sig = 1.0 / (1.0 + jnp.exp(-before))
        hidden = (before / (1.0 + jnp.exp(-before))).astype(BF16)
        hidden_t = hidden.T
        slope = sig * (1.0 + before * (1.0 - sig)) * masks[...]
        slots[0:4] = hidden.astype(F32).reshape(4, 64, 256)
        place(1, 0, fkh)
        third = halo(1, 0)

        second.wait_recv()
        put_halo(0, 1, fkg)
        grad = (conv(fkg, cells, tmats, 3) * slope).astype(BF16)
        slots[0:4] = grad.astype(F32).reshape(4, 64, 256)
        place(1, 1, fkf)
        fourth = halo(1, 1)

        kernel_grad(grad.T, fki, cells, blocks)
        pack_blocks(blocks, pw, 0)
        kernel_grad(hidden_t, fkg, cells, blocks2)
        pack_blocks(blocks2, pw, 224)
        pw[448:480, :] = jnp.zeros((32, 128), BF16)
        pw[480:512, :] = jnp.zeros((32, 128), BF16)
        for k in range(g1):
            p1[k] = pw[rows_w * k : rows_w * k + rows_w, :]
        q1[m] = p1[m]

        def start_all(src, dst, mine, count, peer, send, recv, by_peer):
            slow, fast = (n_r, outer) if peer is peer1 else (g2 // 2, 2)
            steps = [(a, b) for a in range(slow) for b in range(fast) if (a, b) != (0, 0)]
            hops = (lambda b: min(b, fast - b)) if peer is peer1 else (lambda b: 0)
            steps.sort(key=lambda ab: -min(ab[0], slow - ab[0]) - hops(ab[1]))
            for a, b in steps:
                other = (mine // fast + a) % slow * fast + (mine % fast + b) % fast
                pltpu.make_async_remote_copy(
                    src_ref=src.at[other] if by_peer else src,
                    dst_ref=dst.at[mine],
                    send_sem=send,
                    recv_sem=recv,
                    device_id=peer(other),
                    device_id_type=MESH,
                ).start()

        def wait_all(src, dst, mine, count, peer, send, recv, by_peer):
            c = pltpu.make_async_remote_copy(
                src_ref=dst.at[0 : count - 1],
                dst_ref=dst.at[0 : count - 1],
                send_sem=send,
                recv_sem=recv,
                device_id=peer((mine + 1) % count),
                device_id_type=MESH,
            )
            c.wait_recv()
            c.wait_send()

        plan_w1 = (p1, q1, m, g1, peer1, w1s, w1r, True)
        plan_w2 = (p2, q2, u, g2, peer2, w2s, w2r, False)
        plan_w3 = (p3, q3, m, g1, peer1, w3s, w3r, False)
        plan_d1 = (d1, e1, m, g1, peer1, d1s, d1r, True)
        plan_d2 = (d2, e2, u, g2, peer2, d2s, d2r, False)
        plan_d3 = (d3, e3, m, g1, peer1, d3s, d3r, False)

        def added(ref, count):
            total = ref[0].astype(F32)
            for k in range(1, count):
                total = total + ref[k].astype(F32)
            return total

        start_all(*plan_w1)

        third.wait_recv()
        put_halo(1, 0, fkh)
        summed = (inps[...] + conv(fkh, cells, tmats, 1) * masks[...]).reshape(16, 2, 8, 256)
        lhs = jnp.concatenate(
            [summed[:, 0].reshape(128, 256), summed[:, 1].reshape(128, 256)], axis=1
        ).astype(BF16)

        crow_f = crow[...]
        rhs = jnp.concatenate(
            [jnp.where(odd, 0.0, crow_f).astype(BF16), jnp.where(odd, crow_f, 0.0).astype(BF16)], axis=1
        )
        low64 = iota((64, 128), 1) < 64
        for a in range(2):
            mscr[:, 0:512] = mm(lhs[:, 256 * a : 256 * a + 256].T, rhs)
            halves = []
            for d in range(2):
                c0 = 256 * d
                even_part = mscr[0:64, c0 : c0 + 128] + mscr[128:192, c0 + 128 : c0 + 256]
                odd_part = mscr[64:128, c0 : c0 + 128] + mscr[192:256, c0 + 128 : c0 + 256]
                if d == 0:
                    halves.append(even_part + pltpu.roll(odd_part, 64, 1))
                else:
                    halves.append(pltpu.roll(even_part, 64, 1) + odd_part)
            pd[64 * a : 64 * a + 64, :] = jnp.where(low64, halves[0], halves[1])
        for k in range(g1):
            d1[k] = pd[rows_d * k : rows_d * k + rows_d, :].astype(BF16)
        e1[m] = d1[m]
        start_all(*plan_d1)

        rows = mm(lhs, wdn[:, 0:256]) + pltpu.roll(mm(lhs, wdn[:, 256:512]), 127, 0)
        rows = rows.astype(BF16)
        for s in range(4):
            wide = mmd(rows[32 * s : 32 * s + 32, :], even, TN)
            total = None
            for y4 in range(4):
                part = jnp.where(iota((64, 64), 1) // 4 % 4 == y4, wide[64 * y4 : 64 * y4 + 64], 0.0)
                total = part if total is None else total + part
            cots[pl.ds(s, 64, stride=8), :] = jnp.concatenate([total, total], axis=1)
        low4 = iota((4, 128), 1) < 64
        for k in range(32):
            o_down[:, 128 * k : 128 * k + 128] = jnp.where(
                low4, cots[pl.ds(16 * k, 4), :], cots[pl.ds(16 * k + 8, 4), :]
            ).astype(BF16)

        wait_all(*plan_w1)
        p2[...] = added(q1, g1).astype(BF16)
        q2[u] = p2[...]
        start_all(*plan_w2)

        fourth.wait_recv()
        put_halo(1, 1, fkf)
        value = (back[...].reshape(256, 256) + conv(fkf, cells, tmats, 2)) * masks[...]
        value = value.astype(BF16)

        wait_all(*plan_d1)
        d2[...] = added(e1, g1).astype(BF16)
        e2[u] = d2[...]
        start_all(*plan_d2)

        for c in (first, second, third, fourth):
            c.wait_send()
        jl512 = iota((32, 512), 1) // 8 % 8
        for s in range(4):
            wide = mmd(value[64 * s : 64 * s + 64, :], pick[...], TN)
            total = None
            for j in range(8):
                part = jnp.where(jl512 == j, wide[32 * j : 32 * j + 32], 0.0)
                total = part if total is None else total + part
            o_gf[s] = total.astype(BF16)

        wait_all(*plan_w2)
        p3[...] = (added(q2, g2) * scale).astype(BF16)
        q3[m] = p3[...]
        start_all(*plan_w3)
        wait_all(*plan_d2)
        d3[...] = (added(e2, g2) * scale).astype(BF16)
        e3[m] = d3[...]
        start_all(*plan_d3)

        wait_all(*plan_w3)
        for k in range(g1):
            o_pw[rows_w * k : rows_w * k + rows_w, :] = q3[k]
        wait_all(*plan_d3)
        for k in range(g1):
            o_pd[rows_d * k : rows_d * k + rows_d, :] = e3[k].astype(F32)

    def vm(shape, dtype=F32):
        return pltpu.VMEM(shape, dtype)

    dma = pltpu.SemaphoreType.DMA
    field = vm((8, 96, 1024), BF16)
    scratch = [
        pltpu.SMEM((4,), jnp.int32), vm((4, 32, 512), BF16), vm((4, 512), jnp.int32), vm((4, 4096), BF16), vm((2, 27, 32, 32), BF16), vm((8, 32, 64), BF16),
        vm((4, 3, 1024, 256), BF16), vm((4, 896, 128), BF16), vm((512, 512), BF16), vm((256, 1024), BF16),
        vm((64, 512), BF16), vm((5, 64, 256)), vm((128, 256)), vm((512, 128)), vm((256, 256)), vm((256, 256)), vm((16, 2, 8, 256)),
        field, field, field, field, vm((256, 1024)), vm((9, 32, 128)), vm((9, 32, 128)),
        vm((2, 2, 416, 128), BF16), vm((2, 2, 416, 128), BF16),
        vm((512, 128), BF16), vm((g1, rows_w, 128), BF16), vm((g1, rows_w, 128), BF16),
        vm((rows_w, 128), BF16), vm((g2, rows_w, 128), BF16), vm((rows_w, 128), BF16), vm((g1, rows_w, 128), BF16),
        vm((128, 128)), vm((g1, rows_d, 128), BF16), vm((g1, rows_d, 128), BF16),
        vm((rows_d, 128), BF16), vm((g2, rows_d, 128), BF16), vm((rows_d, 128), BF16), vm((g1, rows_d, 128), BF16),
        dma((7,)), dma((2, 2)), dma((2, 2)),
        *[dma] * 12,
    ]
    whole = pl.BlockSpec(memory_space=pltpu.VMEM)
    far = pl.BlockSpec(memory_space=pltpu.HBM)
    step = pl.pallas_call(
        body,
        out_shape=(
            jax.ShapeDtypeStruct((512, 128), BF16),
            jax.ShapeDtypeStruct((128, 128), F32),
            jax.ShapeDtypeStruct((4, 32, 512), BF16),
            jax.ShapeDtypeStruct((4, 4096), BF16),
        ),
        in_specs=[far] * 7,
        out_specs=(whole,) * 4,
        scratch_shapes=scratch,
        compiler_params=pltpu.CompilerParams(
            collective_id=0, has_side_effects=True, vmem_limit_bytes=32 * 1024 * 1024
        ),
    )
    last = pl.pallas_call(
        finish,
        out_shape=(
            jax.ShapeDtypeStruct((4, 4096), BF16),
            jax.ShapeDtypeStruct((4, 32, 512), BF16),
            jax.ShapeDtypeStruct((27, 32, 32), F32),
            jax.ShapeDtypeStruct((27, 32, 32), F32),
            jax.ShapeDtypeStruct((8, 32, 64), F32),
        ),
        in_specs=[whole] * 4,
        out_specs=(whole,) * 5,
        compiler_params=pltpu.CompilerParams(vmem_limit_bytes=8 * 1024 * 1024),
    )

    def on_device(features, voxel_mask, brick_cell, conv_one, conv_two, down_weight, cotangent):
        pw, pd, gf, down = step(
            *[
                pltpu.with_memory_space_constraint(x, pltpu.HBM)
                for x in (brick_cell, features, voxel_mask, cotangent, conv_one, conv_two, down_weight)
            ]
        )
        return last(pw, pd, gf, down)

    return on_device


def solution(mesh):
    rows = P(("region", "tile"), None)
    cube = P(("region", "tile"), None, None)
    in_specs = (cube, rows, P(("region", "tile")), P(), P(), P(), rows)
    out_specs = (rows, cube, P(), P(), P())
    return jax.shard_map(
        build(mesh.shape["region"], mesh.shape["tile"]),
        mesh=mesh,
        in_specs=in_specs,
        out_specs=out_specs,
        check_vma=False,
    )
```

```python
import math

import jax
import jax.numpy as jnp
from jax import lax
from jax.experimental import pallas as pl
from jax.experimental.pallas import tpu as pltpu
from jax.sharding import PartitionSpec as P

MESH = pl.DeviceIdType.MESH
F32 = jnp.float32
BF16 = jnp.bfloat16
NT = (((1,), (1,)), ((), ()))
TN = (((0,), (0,)), ((), ()))


def mm(a, b):
    return jnp.dot(a, b, preferred_element_type=F32)


def mmd(a, b, dims):
    return lax.dot_general(a, b, dims, preferred_element_type=F32)


def iota(shape, dim):
    return lax.broadcasted_iota(jnp.int32, shape, dim)


def one_hot(cond):
    return jnp.where(cond, 1.0, 0.0)


def put(fk, zb, first_x, value, lanes):
    n = value.shape[0] // 8
    for xb in range(2):
        base = 8 * xb
        for a, b in ((base, base + 1), (base + 1, base + 9), (base + 9, base + 10)):
            a, b = max(a, first_x), min(b, first_x + n)
            if a < b:
                part = value[8 * (a - first_x) : 8 * (b - first_x)]
                fk[4 * xb + zb, 8 * (a - base) + 8 : 8 * (b - base) + 8, lanes] = part.astype(BF16)


def put_center(fk, first_x, rows):
    n = rows.shape[0] // 32
    cube = rows.reshape(4 * n, 8, 256)
    down = pltpu.roll(cube, 1, 1).reshape(n, 4, 8, 256)
    up = pltpu.roll(cube, 7, 1).reshape(n, 4, 8, 256)
    cube = cube.reshape(n, 4, 8, 256)
    row = iota((n, 8, 256), 1)
    for zb in range(4):
        below = jnp.where(row > 0, down[:, zb], down[:, zb - 1] if zb > 0 else 0.0)
        above = jnp.where(row < 7, up[:, zb], up[:, zb + 1] if zb < 3 else 0.0)
        for k, part in enumerate((below, cube[:, zb], above)):
            flat = part.reshape(8 * n, 256)
            put(fk, zb, first_x, flat[:, 0:128], slice(128 * k, 128 * k + 128))
            put(fk, zb, first_x, flat[:, 128:256], slice(512 + 128 * k, 640 + 128 * k))


def pack_edge(rows, lane0, lanes):
    n = rows.shape[0] // 32
    cube = rows.reshape(n, 4, 8, 128)
    total = None
    for zb in range(4):
        part = cube[:, zb].reshape(n * 8, 128)
        turn = (32 * zb - lane0) % 128
        if turn:
            part = pltpu.roll(part, turn, 1)
        total = part if total is None else jnp.where(lanes // 32 == zb, part, total)
    return total


def put_edges(fk, first_x, side, packed):
    n = packed.shape[0] // 8
    lane = iota((n * 8, 128), 1)
    row = iota((n * 8, 128), 0) % 8
    cube = packed.reshape(n, 8, 128)
    down = pltpu.roll(cube, 1, 1).reshape(n * 8, 128)
    down = jnp.where(row > 0, down, jnp.where(lane >= 32, pltpu.roll(down, 32, 1), 0.0))
    up = pltpu.roll(cube, 7, 1).reshape(n * 8, 128)
    up = jnp.where(row < 7, up, jnp.where(lane < 96, pltpu.roll(up, 96, 1), 0.0))
    for zb in range(4):
        value = 0.0
        for k, part in ((2, up), (1, packed), (0, down)):
            turn = (32 * k - 32 * zb) % 128
            value = jnp.where(lane < 32 * k + 32, pltpu.roll(part, turn, 1) if turn else part, value)
        at = 512 * side + 384
        put(fk, zb, first_x, value, slice(at, at + 128))


def window(fk, cells, dx):
    return jnp.concatenate([fk[e, 8 * dx + 8 : 8 * dx + 72, :] for e in cells], axis=0)


def conv(fk, cells, t_ref, kind):
    total = None
    for dx in range(3):
        term = mm(window(fk, cells, dx), t_ref[kind, dx])
        total = term if total is None else total + term
    return total


def kernel_grad(xt, fk, cells, blocks):
    lane = iota((32, 128), 1)
    for dx in range(3):
        near = window(fk, cells, dx)
        low = mm(xt[0:160], near[:, 0:512])
        high = mm(xt[96:256], near[:, 512:1024])
        for dz in range(3):
            lo = [low[32 * j : 32 * j + 32, 128 * dz : 128 * dz + 128] for j in range(5)]
            hi = [high[32 * j : 32 * j + 32, 128 * dz : 128 * dz + 128] for j in range(5)]
            still = lo[1] + hi[2]
            back = lo[2] + hi[3]
            half = jnp.where(lane >= 64, lo[3] + hi[4], jnp.where(lane < 32, hi[0], 0.0))
            ahead = jnp.where(lane >= 96, lo[4], jnp.where(lane < 64, hi[1] + lo[0], 0.0))
            mine = lane // 32 == dz
            first = jnp.where(mine, low[0:32, 384:512], 0.0)
            last = jnp.where(mine, high[128:160, 384:512], 0.0)
            if dz == 0:
                still, half = still + first, half + last
            elif dz == 1:
                back, ahead = back + first, ahead + last
            else:
                half, still = half + first, still + last
            blocks[3 * dx + dz] = (
                still + pltpu.roll(back, 96, 1) + pltpu.roll(half, 64, 1) + pltpu.roll(ahead, 32, 1)
            )


def pack_blocks(blocks, dst, first):
    lane = iota((32, 128), 1)
    for g in range(7):
        value = blocks[g]
        if g < 6:
            extra = pltpu.roll(blocks[7 + g // 3], 32 * (3 - g % 3), 1)
            value = jnp.where(lane < 96, value, extra)
        dst[first + 32 * g : first + 32 * g + 32, :] = value.astype(BF16)


def tap_of(group, slot):
    block, dy = (group, slot) if slot < 3 else (7 + group // 3, group % 3)
    return 9 * (block // 3) + 3 * dy + block % 3


def finish(pw, pd, gf, down, o_down, o_gf, o_w1, o_w2, o_wd):
    for g in range(7):
        one = pw[32 * g : 32 * g + 32, :].astype(F32).T
        two = pw[224 + 32 * g : 224 + 32 * g + 32, :].astype(F32)
        for slot in range(4 if g < 6 else 3):
            k = tap_of(g, slot)
            o_w1[k] = one[32 * slot : 32 * slot + 32, :]
            o_w2[26 - k] = two[:, 32 * slot : 32 * slot + 32]
    for a in range(2):
        for b in range(2):
            for d in range(2):
                o_wd[4 * a + 2 * b + d] = pd[64 * a + 32 * b : 64 * a + 32 * b + 32, 64 * d : 64 * d + 64]
    o_gf[...] = gf[...]
    o_down[...] = down[...]


def build(n_r, n_t):
    inner = min(16, n_t)
    outer = n_t // inner
    g1 = n_r * outer
    g2 = inner
    rows_w = 512 // g1
    rows_d = 128 // g1
    scale = 1.0 / math.sqrt(4 * n_r * n_t * 512.0)

    def body(
        bc_h, feat_h, vmask_h, cot_h, one_h, two_h, dw_h,
        o_pw, o_pd, o_gf, o_down,
        bc, feat, vmask, cot, wraw, dw,
        tmats, wtile, wdn, wback, pick, slots, crow, cots, inps, masks, back,
        fki, fkg, fkh, fkf, mscr, blocks, blocks2,
        sbuf, rbuf,
        pw, p1, q1, p2, q2, p3, q3, pd, d1, e1, d2, e2, d3, e3,
        ins, hs, hr, w1s, w1r, w2s, w2r, w3s, w3r, d1s, d1r, d2s, d2r, d3s, d3r,
    ):
        loads = [
            pltpu.make_async_copy(src, dst, ins.at[k])
            for k, (src, dst) in enumerate(
                [(feat_h, feat), (vmask_h, vmask), (cot_h, cot), (dw_h, dw), (one_h, wraw.at[0]), (two_h, wraw.at[1]), (bc_h, bc)]
            )
        ]
        for c in loads:
            c.start()
        r = lax.axis_index("region")
        t = lax.axis_index("tile")
        y = t // inner
        u = t % inner
        m = r * outer + y

        def peer1(k):
            return (k // outer, (k % outer) * inner + u)

        def peer2(k):
            return (r, y * inner + k)

        near = [(dr, dt) for dr in (-1, 0, 1) for dt in (-1, 0, 1) if (dr, dt) != (0, 0)]

        def neighbour(dr, dt):
            return ((r + dr + n_r) % n_r, (t + dt + n_t) % n_t)

        barrier = pltpu.get_barrier_semaphore()
        for dr, dt in near:
            pl.semaphore_signal(barrier, inc=1, device_id=neighbour(dr, dt), device_id_type=MESH)

        def greet1(k, carry):
            pl.semaphore_signal(barrier, inc=1, device_id=peer1((m + k) % g1), device_id_type=MESH)
            return carry

        def greet2(k, carry):
            pl.semaphore_signal(barrier, inc=1, device_id=peer2((u + k) % g2), device_id_type=MESH)
            return carry

        lax.fori_loop(1, g1, greet1, 0)
        lax.fori_loop(1, g2, greet2, 0)

        nothing = jnp.zeros((32, 128), BF16)
        for c in range(2):
            wtile[c, 864:896, :] = nothing
        for kind in range(4):
            for dx in range(3):
                for at in range(0, 1024, 32):
                    high_row = at >= 512
                    inner_row = at % 512 < 384
                    j = at % 128 // 32 + 4 * high_row
                    for half in range(2):
                        pad = at % 512 == 480
                        full = 4 * half - 1 <= j <= 4 * half + 4 if inner_row else half == high_row
                        if pad or not full:
                            tmats[kind, dx, at : at + 32, 128 * half : 128 * half + 128] = nothing

        v = iota((64, 512), 1)
        w = iota((64, 512), 0)
        pick[...] = one_hot((v // 64 == w // 8) & (v % 8 == w % 8)).astype(BF16)
        jlane = iota((32, 128), 1) // 8 % 8
        jmask = [jnp.concatenate([one_hot(jlane == j).astype(BF16)] * 4, axis=1) for j in range(8)]
        jcols = one_hot(iota((64, 256), 0) // 8 == iota((64, 256), 1) // 32).astype(BF16)
        jcols = jnp.concatenate([jcols] * 8, axis=0)
        cv = iota((32, 64), 1)
        cw = iota((32, 64), 0)
        up = one_hot((cv // 16 == cw // 8) & (cv % 4 == cw % 8 // 2)).astype(BF16)
        even = one_hot((cv // 16 == cw // 8) & (2 * (cv % 4) == cw % 8)).astype(BF16)
        ymask = one_hot(iota((256, 64), 1) // 4 % 4 == iota((256, 64), 0) // 64).astype(BF16)
        slots[4] = jnp.zeros((64, 256), F32)

        def halo(phase, field):
            plan = [
                (256, 320, 64, (-1, 0)),
                (320, 256, 64, (1, 0)),
                (0, 128, 128, (0, -1)),
                (128, 0, 128, (0, 1)),
                (384, 408, 8, (-1, -1)),
                (392, 400, 8, (-1, 1)),
                (400, 392, 8, (1, -1)),
                (408, 384, 8, (1, 1)),
            ]
            copies = [
                pltpu.make_async_remote_copy(
                    src_ref=sbuf.at[phase, field, src : src + size],
                    dst_ref=rbuf.at[phase, field, dst : dst + size],
                    send_sem=hs.at[phase, field],
                    recv_sem=hr.at[phase, field],
                    device_id=neighbour(dr, dt),
                    device_id_type=MESH,
                )
                for src, dst, size, (dr, dt) in plan
            ]
            for c in copies:
                c.start()
            return pltpu.make_async_remote_copy(
                src_ref=sbuf.at[phase, field],
                dst_ref=rbuf.at[phase, field],
                send_sem=hs.at[phase, field],
                recv_sem=hr.at[phase, field],
                device_id=neighbour(0, 1),
                device_id_type=MESH,
            )

        def place(phase, field, fk):
            lanes = iota((64, 128), 1)
            for part in range(2):
                rows = jnp.concatenate(
                    [slots[owners[4 * part + zb]].reshape(8, 1, 8, 256) for zb in range(4)], axis=1
                ).reshape(256, 256)
                put_center(fk, 1 + 8 * part, rows)
                low = pack_edge(rows[:, 0:128], 0, lanes)
                high = pack_edge(rows[:, 128:256], 96, lanes)
                sbuf[phase, field, 64 * part : 64 * part + 64, :] = low.astype(BF16)
                sbuf[phase, field, 128 + 64 * part : 192 + 64 * part, :] = high.astype(BF16)
                a = 224 * part
                b = 56 * part
                x = 256 + 64 * part
                sbuf[phase, field, x : x + 32, :] = rows[a : a + 32, 0:128].astype(BF16)
                sbuf[phase, field, x + 32 : x + 64, :] = rows[a : a + 32, 128:256].astype(BF16)
                x = 384 + 16 * part
                sbuf[phase, field, x : x + 8, :] = low[b : b + 8].astype(BF16)
                sbuf[phase, field, x + 8 : x + 16, :] = high[b : b + 8].astype(BF16)

        has = [
            jnp.where(r > 0, 1.0, 0.0),
            jnp.where(r < n_r - 1, 1.0, 0.0),
            jnp.where(t > 0, 1.0, 0.0),
            jnp.where(t < n_t - 1, 1.0, 0.0),
        ]

        def put_halo(phase, field, fk):
            for end in range(2):
                x = 256 + 64 * end
                plane = jnp.concatenate(
                    [rbuf[phase, field, x : x + 32, :], rbuf[phase, field, x + 32 : x + 64, :]], axis=1
                )
                put_center(fk, 17 * end, plane.astype(F32) * has[end])
            for side in range(2):
                face = rbuf[phase, field, 128 * side : 128 * side + 128, :]
                put_edges(fk, 1, side, face.astype(F32) * has[2 + side])
                for end in range(2):
                    x = 384 + 16 * end + 8 * side
                    packed = rbuf[phase, field, x : x + 8, :].astype(F32)
                    put_edges(fk, 17 * end, side, packed * (has[end] * has[2 + side]))

        loads[6].wait()
        cells = [jnp.maximum(bc[s], 0) for s in range(4)]
        lives = [jnp.where(bc[s] >= 0, 1.0, 0.0) for s in range(4)]
        owners = []
        for e in range(8):
            owner = jnp.int32(4)
            for s in range(4):
                owner = jnp.where(bc[s] == e, jnp.int32(s), owner)
            owners.append(owner)

        loads[0].wait()
        loads[1].wait()
        for s in range(4):
            seen = jnp.broadcast_to((vmask[s : s + 1, :].astype(F32) * lives[s]), (64, 512)).astype(BF16)
            masks[64 * s : 64 * s + 64, :] = mm(pick[...] * seen, jcols)
            kept = feat[s] * seen[0:32]
            tall = jnp.concatenate([kept * jmask[j] for j in range(8)], axis=0)
            got = mmd(pick[...], tall, NT)
            inps[64 * s : 64 * s + 64, :] = got
            slots[s] = got
        place(0, 0, fki)
        pl.semaphore_wait(barrier, 8 + (g1 - 1) + (g2 - 1))
        first = halo(0, 0)

        loads[2].wait()
        loads[3].wait()
        dwide = dw[...].reshape(256, 64).astype(F32)
        dtile = jnp.concatenate([dwide, dwide], axis=1)
        lane64 = iota((32, 128), 1) // 64
        for a in range(2):
            for b in range(2):
                for d in range(2):
                    k = 4 * a + 2 * b + d
                    block = dtile[32 * k : 32 * k + 32]
                    for y4 in range(4):
                        row = 256 * a + 32 * (2 * y4 + b)
                        for half in range(2):
                            col = 256 * d + 128 * half
                            if y4 // 2 == half:
                                value = jnp.where(lane64 == y4 % 2, block, 0.0).astype(BF16)
                            else:
                                value = jnp.zeros((32, 128), BF16)
                            wdn[row : row + 32, col : col + 128] = value
        lane32 = iota((64, 128), 1)
        for a in range(2):
            turned = dtile[128 * a : 128 * a + 128, :].T[0:64]
            for d in range(2):
                low = turned if d == 0 else pltpu.roll(turned, 96, 1)
                high = pltpu.roll(turned, 96 - 32 * d, 1)
                pair = jnp.where(lane32 < 32, low, jnp.where(lane32 < 64, high, 0.0))
                pair = pair + pltpu.roll(pair, 64, 1)
                for y4 in range(4):
                    for half in range(2):
                        col = 512 * a + 256 * d + 128 * half
                        if y4 // 2 == half:
                            value = jnp.where(lane32 // 64 == y4 % 2, pair, 0.0).astype(BF16)
                        else:
                            value = jnp.zeros((64, 128), BF16)
                        wback[64 * y4 : 64 * y4 + 64, col : col + 128] = value

        for k in range(32):
            part = cot[:, 128 * k : 128 * k + 128].astype(F32)
            cots[pl.ds(16 * k, 4), :] = part
            cots[pl.ds(16 * k + 8, 4), :] = pltpu.roll(part, 64, 1)
        for s in range(4):
            native = cots[pl.ds(s, 64, stride=8), :][:, 0:64].astype(BF16)
            tall = jnp.concatenate([native] * 4, axis=0) * ymask
            crow[32 * s : 32 * s + 32, :] = mmd(up, tall, NT)
        crow_b = crow[...].astype(BF16)
        odd = iota((128, 256), 0) % 2 == 1
        for a in range(2):
            back[:, a] = jnp.where(
                odd,
                mm(crow_b, wback[:, 512 * a + 256 : 512 * a + 512]),
                mm(crow_b, wback[:, 512 * a : 512 * a + 256]),
            ).reshape(16, 8, 256)
        for s in range(4):
            rows = back[4 * s : 4 * s + 4].reshape(64, 256) * masks[64 * s : 64 * s + 64, :]
            slots[s] = rows.astype(BF16).astype(F32)
        place(0, 1, fkg)
        second = halo(0, 1)

        loads[4].wait()
        loads[5].wait()
        gap = jnp.zeros((864, 96), BF16)
        for c in range(2):
            flat = jnp.concatenate([wraw[c].reshape(864, 32), gap], axis=1)
            flat = flat + pltpu.roll(flat, 32, 1)
            wtile[c, 0:864, :] = flat + pltpu.roll(flat, 64, 1)
        lane = iota((32, 128), 1)
        quarter = [one_hot(lane // 32 == k).astype(BF16) for k in range(4)]
        quarter4 = [jnp.concatenate([q] * 4, axis=0) for q in quarter]

        def transpose_taps(c):
            for pack in range(2):
                groups = range(4 * pack, min(4 * pack + 4, 7))
                value = None
                for g in groups:
                    term = wtile[c, 128 * g : 128 * g + 128, :] * quarter4[g % 4]
                    value = term if value is None else value + term
                turned = value.T
                for g in groups:
                    mine = turned[32 * (g % 4) : 32 * (g % 4) + 32]
                    for k in range(4 if g < 6 else 3):
                        piece = mine * quarter[k]
                        piece = piece + pltpu.roll(piece, 32, 1)
                        at = 32 * (26 - 4 * g - k)
                        wtile[2 + c, at : at + 32, :] = piece + pltpu.roll(piece, 64, 1)

        transpose_taps(1)

        def band(kind, carry):
            for dx in range(3):
                for dz in range(3):
                    low, mid, high = (
                        wtile[kind, 32 * (9 * dx + 3 * dy + dz) : 32 * (9 * dx + 3 * dy + dz) + 32, :]
                        for dy in range(3)
                    )
                    for j in range(8):
                        at = 512 * (j // 4) + 128 * dz + 32 * (j % 4)
                        for half in range(2):
                            value = None
                            for jo, tap in ((j - 1, high), (j, mid), (j + 1, low)):
                                if 4 * half <= jo < 4 * half + 4:
                                    term = tap * quarter[jo - 4 * half]
                                    value = term if value is None else value + term
                            if value is not None:
                                tmats[kind, dx, at : at + 32, 128 * half : 128 * half + 128] = value
                    at = 384 + 32 * dz
                    tmats[kind, dx, at : at + 32, 0:128] = low * quarter[0]
                    tmats[kind, dx, at + 512 : at + 544, 128:256] = high * quarter[3]
            return carry

        lax.fori_loop(0, 2, band, 0)
        band(3, 0)

        first.wait_recv()
        put_halo(0, 0, fki)
        before = conv(fki, cells, tmats, 0) * masks[...]
        sig = 1.0 / (1.0 + jnp.exp(-before))
        hidden = (before / (1.0 + jnp.exp(-before))).astype(BF16)
        hidden_t = hidden.T
        slope = sig * (1.0 + before * (1.0 - sig)) * masks[...]
        slots[0:4] = hidden.astype(F32).reshape(4, 64, 256)
        place(1, 0, fkh)
        third = halo(1, 0)

        second.wait_recv()
        put_halo(0, 1, fkg)
        grad = (conv(fkg, cells, tmats, 3) * slope).astype(BF16)
        slots[0:4] = grad.astype(F32).reshape(4, 64, 256)
        place(1, 1, fkf)
        fourth = halo(1, 1)

        kernel_grad(grad.T, fki, cells, blocks)
        pack_blocks(blocks, pw, 0)
        kernel_grad(hidden_t, fkg, cells, blocks2)
        pack_blocks(blocks2, pw, 224)
        pw[448:480, :] = jnp.zeros((32, 128), BF16)
        pw[480:512, :] = jnp.zeros((32, 128), BF16)
        for k in range(g1):
            p1[k] = pw[rows_w * k : rows_w * k + rows_w, :]
        q1[m] = p1[m]

        def start_all(src, dst, mine, count, peer, send, recv, by_peer):
            slow, fast = (n_r, outer) if peer is peer1 else (g2 // 2, 2)
            steps = [(a, b) for a in range(slow) for b in range(fast) if (a, b) != (0, 0)]
            hops = (lambda b: min(b, fast - b)) if peer is peer1 else (lambda b: 0)
            steps.sort(key=lambda ab: -min(ab[0], slow - ab[0]) - hops(ab[1]))
            for a, b in steps:
                other = (mine // fast + a) % slow * fast + (mine % fast + b) % fast
                pltpu.make_async_remote_copy(
                    src_ref=src.at[other] if by_peer else src,
                    dst_ref=dst.at[mine],
                    send_sem=send,
                    recv_sem=recv,
                    device_id=peer(other),
                    device_id_type=MESH,
                ).start()

        def wait_all(src, dst, mine, count, peer, send, recv, by_peer):
            c = pltpu.make_async_remote_copy(
                src_ref=dst.at[0 : count - 1],
                dst_ref=dst.at[0 : count - 1],
                send_sem=send,
                recv_sem=recv,
                device_id=peer((mine + 1) % count),
                device_id_type=MESH,
            )
            c.wait_recv()
            c.wait_send()

        plan_w1 = (p1, q1, m, g1, peer1, w1s, w1r, True)
        plan_w2 = (p2, q2, u, g2, peer2, w2s, w2r, False)
        plan_w3 = (p3, q3, m, g1, peer1, w3s, w3r, False)
        plan_d1 = (d1, e1, m, g1, peer1, d1s, d1r, True)
        plan_d2 = (d2, e2, u, g2, peer2, d2s, d2r, False)
        plan_d3 = (d3, e3, m, g1, peer1, d3s, d3r, False)

        def added(ref, count):
            total = ref[0].astype(F32)
            for k in range(1, count):
                total = total + ref[k].astype(F32)
            return total

        start_all(*plan_w1)

        third.wait_recv()
        put_halo(1, 0, fkh)
        summed = (inps[...] + conv(fkh, cells, tmats, 1) * masks[...]).reshape(16, 2, 8, 256)
        lhs = jnp.concatenate(
            [summed[:, 0].reshape(128, 256), summed[:, 1].reshape(128, 256)], axis=1
        ).astype(BF16)

        crow_f = crow[...]
        rhs = jnp.concatenate(
            [jnp.where(odd, 0.0, crow_f).astype(BF16), jnp.where(odd, crow_f, 0.0).astype(BF16)], axis=1
        )
        low64 = iota((64, 128), 1) < 64
        for a in range(2):
            mscr[:, 0:512] = mm(lhs[:, 256 * a : 256 * a + 256].T, rhs)
            halves = []
            for d in range(2):
                c0 = 256 * d
                even_part = mscr[0:64, c0 : c0 + 128] + mscr[128:192, c0 + 128 : c0 + 256]
                odd_part = mscr[64:128, c0 : c0 + 128] + mscr[192:256, c0 + 128 : c0 + 256]
                if d == 0:
                    halves.append(even_part + pltpu.roll(odd_part, 64, 1))
                else:
                    halves.append(pltpu.roll(even_part, 64, 1) + odd_part)
            pd[64 * a : 64 * a + 64, :] = jnp.where(low64, halves[0], halves[1])
        for k in range(g1):
            d1[k] = pd[rows_d * k : rows_d * k + rows_d, :].astype(BF16)
        e1[m] = d1[m]
        start_all(*plan_d1)

        rows = mm(lhs, wdn[:, 0:256]) + pltpu.roll(mm(lhs, wdn[:, 256:512]), 127, 0)
        rows = rows.astype(BF16)
        for s in range(4):
            wide = mmd(rows[32 * s : 32 * s + 32, :], even, TN)
            total = None
            for y4 in range(4):
                part = jnp.where(iota((64, 64), 1) // 4 % 4 == y4, wide[64 * y4 : 64 * y4 + 64], 0.0)
                total = part if total is None else total + part
            cots[pl.ds(s, 64, stride=8), :] = jnp.concatenate([total, total], axis=1)
        low4 = iota((4, 128), 1) < 64
        for k in range(32):
            o_down[:, 128 * k : 128 * k + 128] = jnp.where(
                low4, cots[pl.ds(16 * k, 4), :], cots[pl.ds(16 * k + 8, 4), :]
            ).astype(BF16)

        wait_all(*plan_w1)
        p2[...] = added(q1, g1).astype(BF16)
        q2[u] = p2[...]
        start_all(*plan_w2)
        transpose_taps(0)
        band(2, 0)

        wait_all(*plan_d1)
        d2[...] = added(e1, g1).astype(BF16)
        e2[u] = d2[...]
        start_all(*plan_d2)

        fourth.wait_recv()
        put_halo(1, 1, fkf)
        value = (back[...].reshape(256, 256) + conv(fkf, cells, tmats, 2)) * masks[...]
        value = value.astype(BF16)


        for c in (first, second, third, fourth):
            c.wait_send()
        jl512 = iota((32, 512), 1) // 8 % 8
        for s in range(4):
            wide = mmd(value[64 * s : 64 * s + 64, :], pick[...], TN)
            total = None
            for j in range(8):
                part = jnp.where(jl512 == j, wide[32 * j : 32 * j + 32], 0.0)
                total = part if total is None else total + part
            o_gf[s] = total.astype(BF16)

        wait_all(*plan_w2)
        p3[...] = (added(q2, g2) * scale).astype(BF16)
        q3[m] = p3[...]
        start_all(*plan_w3)
        wait_all(*plan_d2)
        d3[...] = (added(e2, g2) * scale).astype(BF16)
        e3[m] = d3[...]
        start_all(*plan_d3)

        wait_all(*plan_w3)
        for k in range(g1):
            o_pw[rows_w * k : rows_w * k + rows_w, :] = q3[k]
        wait_all(*plan_d3)
        for k in range(g1):
            o_pd[rows_d * k : rows_d * k + rows_d, :] = e3[k].astype(F32)

    def vm(shape, dtype=F32):
        return pltpu.VMEM(shape, dtype)

    dma = pltpu.SemaphoreType.DMA
    field = vm((8, 96, 1024), BF16)
    scratch = [
        pltpu.SMEM((4,), jnp.int32), vm((4, 32, 512), BF16), vm((4, 512), jnp.int32), vm((4, 4096), BF16), vm((2, 27, 32, 32), BF16), vm((8, 32, 64), BF16),
        vm((4, 3, 1024, 256), BF16), vm((4, 896, 128), BF16), vm((512, 512), BF16), vm((256, 1024), BF16),
        vm((64, 512), BF16), vm((5, 64, 256)), vm((128, 256)), vm((512, 128)), vm((256, 256)), vm((256, 256)), vm((16, 2, 8, 256)),
        field, field, field, field, vm((256, 1024)), vm((9, 32, 128)), vm((9, 32, 128)),
        vm((2, 2, 416, 128), BF16), vm((2, 2, 416, 128), BF16),
        vm((512, 128), BF16), vm((g1, rows_w, 128), BF16), vm((g1, rows_w, 128), BF16),
        vm((rows_w, 128), BF16), vm((g2, rows_w, 128), BF16), vm((rows_w, 128), BF16), vm((g1, rows_w, 128), BF16),
        vm((128, 128)), vm((g1, rows_d, 128), BF16), vm((g1, rows_d, 128), BF16),
        vm((rows_d, 128), BF16), vm((g2, rows_d, 128), BF16), vm((rows_d, 128), BF16), vm((g1, rows_d, 128), BF16),
        dma((7,)), dma((2, 2)), dma((2, 2)),
        *[dma] * 12,
    ]
    whole = pl.BlockSpec(memory_space=pltpu.VMEM)
    far = pl.BlockSpec(memory_space=pltpu.HBM)
    step = pl.pallas_call(
        body,
        out_shape=(
            jax.ShapeDtypeStruct((512, 128), BF16),
            jax.ShapeDtypeStruct((128, 128), F32),
            jax.ShapeDtypeStruct((4, 32, 512), BF16),
            jax.ShapeDtypeStruct((4, 4096), BF16),
        ),
        in_specs=[far] * 7,
        out_specs=(whole,) * 4,
        scratch_shapes=scratch,
        compiler_params=pltpu.CompilerParams(
            collective_id=0, has_side_effects=True, vmem_limit_bytes=32 * 1024 * 1024
        ),
    )
    last = pl.pallas_call(
        finish,
        out_shape=(
            jax.ShapeDtypeStruct((4, 4096), BF16),
            jax.ShapeDtypeStruct((4, 32, 512), BF16),
            jax.ShapeDtypeStruct((27, 32, 32), F32),
            jax.ShapeDtypeStruct((27, 32, 32), F32),
            jax.ShapeDtypeStruct((8, 32, 64), F32),
        ),
        in_specs=[whole] * 4,
        out_specs=(whole,) * 5,
        compiler_params=pltpu.CompilerParams(vmem_limit_bytes=8 * 1024 * 1024),
    )

    def on_device(features, voxel_mask, brick_cell, conv_one, conv_two, down_weight, cotangent):
        pw, pd, gf, down = step(
            *[
                pltpu.with_memory_space_constraint(x, pltpu.HBM)
                for x in (brick_cell, features, voxel_mask, cotangent, conv_one, conv_two, down_weight)
            ]
        )
        return last(pw, pd, gf, down)

    return on_device


def solution(mesh):
    rows = P(("region", "tile"), None)
    cube = P(("region", "tile"), None, None)
    in_specs = (cube, rows, P(("region", "tile")), P(), P(), P(), rows)
    out_specs = (rows, cube, P(), P(), P())
    return jax.shard_map(
        build(mesh.shape["region"], mesh.shape["tile"]),
        mesh=mesh,
        in_specs=in_specs,
        out_specs=out_specs,
        check_vma=False,
    )
```
